128 devices in a mesh: rows: 32 (over y, x, core), cls: 4 (over z).
Axes of the slice: x: 4, y: 4, z: 4, core: 2. Of those that a mesh axis runs over, the one named last changes fastest.
Arguments:
- data: bfloat16 [65536, 512], P('rows'), may hold values from -4 to 4
- projections: bfloat16 [512, 1536], replicated, may hold values from -1 to 1
- phases: float32 [1536], replicated, may hold values from -4 to 4
- targets: bfloat16 [65536, 1024], P('rows', 'cls'), may hold values from -8 to 8
- bounds: float32 [3, 2], replicated, may hold values from 0 to 4, as said below
- order: int32 [3], replicated, may hold values from 0 to 2, each once
Outputs:
- weights: float32 [3, 512, 1024], P(None, 'rows', 'cls')
- residual: float32 [65536, 1024], P('rows', 'cls')
The draws below stay inside these ranges and needn't reach their ends.
Inputs may be any that keep to these rules, and one draw needn't show every extreme that they name: bounds[j, 1] is at least the largest eigenvalue of block j's gram, and bounds[j, 1] > bounds[j, 0] > 0. order names each block index once.
All inputs are finite; a program needn't handle non-finite values.
Results may differ from the reference program's by a relative error of at most 0.0014.
Values may be sent and summed in bfloat16 or wider, within the bound.
A program may use at most 64 MiB of HBM per device.

```python
import math
import jax
import jax.numpy as jnp
from jax import lax

DIN = 512
F = 512
C = 1024
NBLK = 3
ITERS = 16
NTOT = 65536


def draw_inputs(key):
    data_key = jax.random.fold_in(key, 101)
    data = jnp.clip(jax.random.normal(data_key, (NTOT, DIN), jnp.float32), -4.0, 4.0)
    data = data.astype(jnp.bfloat16)
    project_key = jax.random.fold_in(key, 202)
    limit = 4.0 / math.sqrt(DIN)
    projections = jax.random.normal(project_key, (DIN, NBLK * F), jnp.float32) / math.sqrt(DIN)
    projections = jnp.clip(projections, -limit, limit).astype(jnp.bfloat16)
    phase_key = jax.random.fold_in(key, 303)
    phases = jax.random.uniform(phase_key, (NBLK * F,), jnp.float32, -math.pi, math.pi)
    return (data, projections, phases)


def block_features(data, projections, phases, block):
    angles = jnp.dot(data, projections[:, block * F:(block + 1) * F], preferred_element_type=jnp.float32)
    return math.sqrt(2.0 / F) * jnp.cos(angles + phases[None, block * F:(block + 1) * F])


def draw_data(key, part):
    return draw_inputs(key)[0]


def draw_projections(key, part):
    return draw_inputs(key)[1]


def draw_phases(key, part):
    return draw_inputs(key)[2]


def draw_targets(key, part):
    data, projections, phases = draw_inputs(key)
    teacher_key = jax.random.fold_in(key, 404)
    noise_key = jax.random.fold_in(key, 707)
    teacher = 0.5 * jax.random.normal(teacher_key, (NBLK * F, C), jnp.float32)
    signal = jnp.zeros((NTOT, C), jnp.float32)
    for block in range(NBLK):
        features = block_features(data, projections, phases, block)
        signal = signal + jnp.dot(features, teacher[block * F:(block + 1) * F], preferred_element_type=jnp.float32)
    noise = 0.5 * jax.random.normal(noise_key, (NTOT, C), jnp.float32)
    return jnp.clip(signal + noise, -8.0, 8.0).astype(jnp.bfloat16)


def draw_bounds(key, part):
    data, projections, phases = draw_inputs(key)
    ridge_key = jax.random.fold_in(key, 505)
    stretch_key = jax.random.fold_in(key, 606)
    ridges = jnp.exp(jax.random.uniform(ridge_key, (NBLK,), jnp.float32, math.log(0.002), math.log(0.01)))
    stretch = jnp.exp(jax.random.uniform(stretch_key, (NBLK,), jnp.float32, math.log(1.05), math.log(1.6)))
    uppers = []
    for block in range(NBLK):
        features = block_features(data, projections, phases, block)
        trace = jnp.sum(features * features) / NTOT
        uppers.append(ridges[block] + stretch[block] * trace + 0.01)
    return jnp.stack([ridges, jnp.stack(uppers)], axis=1).astype(jnp.float32)


def setup_inputs(seed: int = 0) -> dict:
    streams_of = jax.random.split(jax.random.key(seed), 7)
    data = draw_data(jax.random.fold_in(streams_of[6], 71), 0)
    projections = draw_projections(jax.random.fold_in(streams_of[6], 71), 0)
    phases = draw_phases(jax.random.fold_in(streams_of[6], 71), 0)
    targets = draw_targets(jax.random.fold_in(streams_of[6], 71), 0)
    bounds = draw_bounds(jax.random.fold_in(streams_of[6], 71), 0)
    order = jax.random.permutation(streams_of[5], NBLK).astype(jnp.int32)
    return dict(data=data, projections=projections, phases=phases, targets=targets, bounds=bounds, order=order)


def cosine_features(data, projections, phases, block):
    offset = (block * F).astype(jnp.int32)
    columns = lax.dynamic_slice_in_dim(projections, offset, F, 1)
    shifts = lax.dynamic_slice_in_dim(phases, offset, F, 0)
    angles = jnp.dot(data, columns, preferred_element_type=jnp.float32) + shifts[None, :]
    return (math.sqrt(2.0 / F) * jnp.cos(angles)).astype(jnp.bfloat16)

def chebyshev(apply_gram, moment, lower, upper):
    center = 0.5 * (upper + lower)
    half = 0.5 * (upper - lower)
    sigma = center / half
    direction = moment / center

    def advance(index, carry):
        solution, remain, direction, ratio_old = carry
        remain = remain - apply_gram(direction)
        ratio_new = 1.0 / (2.0 * sigma - ratio_old)
        direction = ratio_new * ratio_old * direction + 2.0 * ratio_new / half * remain
        return (solution + direction, remain, direction, ratio_new)
    final = lax.fori_loop(0, ITERS - 1, advance, (direction, moment, direction, 1.0 / sigma))
    return final[0]

def reference(data, projections, phases, targets, bounds, order):
    residual = targets.astype(jnp.float32)
    weights = jnp.zeros((NBLK, F, C), jnp.float32)
    for turn in range(NBLK):
        block = order[turn].astype(jnp.int32)
        features = cosine_features(data, projections, phases, block)
        residual_half = residual.astype(jnp.bfloat16)
        lower = bounds[block, 0]
        upper = bounds[block, 1]
        gram = jnp.dot(features.T, features, preferred_element_type=jnp.float32) / NTOT
        gram = gram + lower * jnp.eye(F, dtype=jnp.float32)
        moment = jnp.dot(features.T, residual_half, preferred_element_type=jnp.float32) / NTOT

        def apply_gram(direction):
            return jnp.dot(gram, direction, precision=lax.Precision.HIGHEST, preferred_element_type=jnp.float32)
        solution = chebyshev(apply_gram, moment, lower, upper)
        weights = lax.dynamic_update_slice(weights, solution[None], (block, jnp.int32(0), jnp.int32(0)))
        solution_half = solution.astype(jnp.bfloat16)
        residual = residual - jnp.dot(features, solution_half, preferred_element_type=jnp.float32)
    return (weights, residual)
```

```python
import functools
import math

import jax
import jax.numpy as jnp
from jax import lax
from jax.experimental import pallas as pl
from jax.experimental.pallas import tpu as pltpu
from jax.sharding import PartitionSpec as P

F = 512
NBLK = 3
TILE = 256
SLAB = 16
BF = jnp.bfloat16
F32 = jnp.float32
TURN = 1.0 / (2.0 * math.pi)


def sine_coefficients(scale):
    import numpy as np

    nodes = np.cos((np.arange(64) + 0.5) * math.pi / 64)
    u = (nodes + 1) / 2 / 16
    a = np.sqrt(u)
    fit = np.polynomial.polynomial.polyfit(u, np.sin(2 * math.pi * a) / a, 4)
    return [float(c) * scale for c in fit]


def scaled_cosine(turns, coefficients):
    whole = jnp.round(turns)
    a = 0.25 - jnp.abs(turns - whole)
    u = a * a
    value = coefficients[-1]
    for c in coefficients[-2::-1]:
        value = value * u + c
    return value * a


def split(x):
    high = x.astype(BF)
    return high, (x - high.astype(F32)).astype(BF)


def dot3(left, right, dims=(((1,), (0,)), ((), ()))):
    lh, ll = left
    rh, rl = right
    dot = functools.partial(lax.dot_general, dimension_numbers=dims, preferred_element_type=F32)
    return dot(lh, rh) + (dot(lh, rl) + dot(ll, rh))


def features_kernel(coefficients, index, data, p0, p1, p2, h0, h1, h2, targets, feats, s_out, m_out, held):
    step = pl.program_id(0)

    @pl.when(step == 0)
    def _():
        s_out[...] = jnp.zeros_like(s_out)
        m_out[...] = jnp.zeros_like(m_out)

    x = data[...]
    y = targets[...]
    contract = (((0,), (0,)), ((), ()))
    for j, (p, h) in enumerate(((p0, h0), (p1, h1), (p2, h2))):
        angle = jnp.dot(x, p[...], preferred_element_type=F32)
        turns = angle * TURN + h[0] * TURN
        f = scaled_cosine(turns, coefficients).astype(BF)
        held[j] = f
        feats[:, j * F:(j + 1) * F] = f
        m_out[j * F:(j + 1) * F, :] += lax.dot_general(f, y, contract, preferred_element_type=F32)
    left = held[index[3]]
    other = held[index[4]]
    s_out[:, :F] += lax.dot_general(left, left, contract, preferred_element_type=F32)
    s_out[:, F:] += lax.dot_general(left, other, contract, preferred_element_type=F32)


def features_call(index, data, projections, phases, targets):
    rows = data.shape[0]
    classes = targets.shape[1]
    kernel = functools.partial(features_kernel, sine_coefficients(math.sqrt(2.0 / F)))

    def columns(j):
        return pl.BlockSpec((data.shape[1], F), lambda i, n: (0, n[j]))

    def shift(j):
        return pl.BlockSpec((1, 1, F), lambda i, n: (n[j], 0, 0))

    return pl.pallas_call(
        kernel,
        grid_spec=pltpu.PrefetchScalarGridSpec(
            num_scalar_prefetch=1,
            grid=(rows // TILE,),
            in_specs=[
                pl.BlockSpec((TILE, data.shape[1]), lambda i, n: (i, 0)),
                *[columns(j) for j in range(NBLK)],
                *[shift(j) for j in range(NBLK)],
                pl.BlockSpec((TILE, classes), lambda i, n: (i, 0)),
            ],
            out_specs=[
                pl.BlockSpec((TILE, NBLK * F), lambda i, n: (i, 0)),
                pl.BlockSpec((F, 2 * F), lambda i, n: (0, 0)),
                pl.BlockSpec((NBLK * F, classes), lambda i, n: (0, 0)),
            ],
            scratch_shapes=[pltpu.VMEM((NBLK, TILE, F), BF)],
        ),
        out_shape=[
            jax.ShapeDtypeStruct((rows, NBLK * F), BF),
            jax.ShapeDtypeStruct((F, 2 * F), F32),
            jax.ShapeDtypeStruct((NBLK * F, classes), F32),
        ],
        name="features",
    )(index, data, *[projections] * 3, *[phases.reshape(NBLK, 1, F)] * 3, targets)


def slabs_body(index, scale, s, out, s4):
    eye = (
        lax.broadcasted_iota(jnp.int32, (F, F), 0) == lax.broadcasted_iota(jnp.int32, (F, F), 1)
    ).astype(F32)
    first = s[:, :F] * scale[0] + eye * scale[1]
    part1 = split(first)
    second = scale[2] * (2.0 * first - dot3(part1, part1))
    part2 = split(second)
    fourth = scale[3] * (2.0 * second - dot3(part2, part2))
    part4 = split(fourth)
    s4[...] = fourth
    slab = s4[pl.ds(pl.multiple_of(index[0] * SLAB, SLAB), SLAB), :]
    row = lax.broadcasted_iota(jnp.int32, (SLAB, F), 0) + index[0] * SLAB
    column = lax.broadcasted_iota(jnp.int32, (SLAB, F), 1)
    unit = (row == column).astype(F32)
    eighth = scale[4] * (2.0 * slab - dot3(split(slab), part4))
    value = scale[5] * (2.0 * unit - eighth)
    value = scale[4] * (2.0 * value - dot3(split(value), part4))
    value = scale[3] * (2.0 * value - dot3(split(value), part2))
    value = scale[2] * (2.0 * value - dot3(split(value), part1))
    value = value * scale[6]
    out[0] = value
    out[1] = dot3(split(value), split(s[:, F:])) * scale[7]


def slabs_call(index, scale, s):
    smem = pl.BlockSpec(memory_space=pltpu.SMEM)
    return pl.pallas_call(
        slabs_body,
        in_specs=[smem, smem, pl.BlockSpec(memory_space=pltpu.VMEM)],
        out_specs=pl.BlockSpec(memory_space=pltpu.VMEM),
        out_shape=jax.ShapeDtypeStruct((2, SLAB, F), F32),
        scratch_shapes=[pltpu.VMEM((F, F), F32)],
        name="slabs",
    )(index, scale, s)


def solve_scales(lower, upper, total):
    center = 0.5 * (upper + lower)
    u = 0.5 * (upper - lower) / center
    factors = []
    for _ in range(4):
        factors.append(2.0 / (2.0 - u * u))
        u = u * u / (2.0 - u * u)
    return jnp.stack(
        [1.0 / (center * total), lower / center, *factors, 1.0 / center, jnp.full((), 1.0 / total, F32)]
    )


def body(data, projections, phases, targets, bounds, order):
    total = data.shape[0] * lax.axis_size("rows")
    me = lax.axis_index("rows").astype(jnp.int32)
    plane = lax.axis_index("cls").astype(jnp.int32)
    left = jnp.minimum(plane, 2)
    other = jnp.maximum(plane - 2, 0)
    index = jnp.concatenate([order.astype(jnp.int32), left[None], other[None]])
    feats, s, m = features_call(index, data, projections, phases, targets)
    s, m = lax.psum((s, m), "rows")
    bound = bounds[order[left]]
    scale = solve_scales(bound[0], bound[1], total)
    slabs = slabs_call(me[None], scale, s)
    slabs = lax.all_gather(slabs, "cls")
    m = (m * (1.0 / total)).reshape(NBLK, F, -1)
    dot = functools.partial(jnp.dot, precision=lax.Precision.HIGHEST, preferred_element_type=F32)
    gather = lambda w: lax.all_gather(w.astype(BF), "rows", axis=0, tiled=True)
    w0 = dot(slabs[0, 0], m[0])
    h0 = gather(w0)
    w1 = dot(slabs[1, 0], m[1]) - dot(slabs[1, 1], h0.astype(F32))
    h1 = gather(w1)
    w2 = dot(slabs[2, 0], m[2]) - dot(slabs[2, 1], h0.astype(F32)) - dot(slabs[3, 1], h1.astype(F32))
    h2 = gather(w2)
    half = jnp.concatenate([h0, h1, h2], axis=0)
    residual = targets.astype(F32) - jnp.dot(feats, half, preferred_element_type=F32)
    weights = jnp.zeros((NBLK,) + w0.shape, F32)
    for turn, w in enumerate((w0, w1, w2)):
        weights = lax.dynamic_update_slice(weights, w[None], (order[turn], jnp.int32(0), jnp.int32(0)))
    return (weights, residual)


def solution(mesh):
    return jax.shard_map(
        body,
        mesh=mesh,
        in_specs=(P("rows", None), P(), P(), P("rows", "cls"), P(), P()),
        out_specs=(P(None, "rows", "cls"), P("rows", "cls")),
        check_vma=False,
    )
```

```python
import functools
import math

import jax
import jax.numpy as jnp
from jax import lax
from jax.experimental import pallas as pl
from jax.experimental.pallas import tpu as pltpu
from jax.sharding import PartitionSpec as P

F = 512
NBLK = 3
TILE = 256
SLAB = 16
BF = jnp.bfloat16
F32 = jnp.float32
LANES = 128
ROWS = 32
PLANES = 4
GRAM, CROSS, MOMENT, HEIGHT = 0, 4 * F, 8 * F, 14 * F
TURN = 1.0 / (2.0 * math.pi)


def sine_coefficients(scale):
    import numpy as np

    nodes = np.cos((np.arange(64) + 0.5) * math.pi / 64)
    u = (nodes + 1) / 2 / 16
    a = np.sqrt(u)
    fit = np.polynomial.polynomial.polyfit(u, np.sin(2 * math.pi * a) / a, 4)
    return [float(c) * scale for c in fit]


def scaled_cosine(turns, coefficients):
    whole = jnp.round(turns)
    a = 0.25 - jnp.abs(turns - whole)
    u = a * a
    value = coefficients[-1]
    for c in coefficients[-2::-1]:
        value = value * u + c
    return value * a


def split(x):
    high = x.astype(BF)
    return high, (x - high.astype(F32)).astype(BF)


def dot3(left, right, dims=(((1,), (0,)), ((), ()))):
    lh, ll = left
    rh, rl = right
    dot = functools.partial(lax.dot_general, dimension_numbers=dims, preferred_element_type=F32)
    return dot(lh, rh) + (dot(lh, rl) + dot(ll, rh))


def features_kernel(coefficients, index, data, p0, p1, p2, h0, h1, h2, targets, feats, sums, held):
    step = pl.program_id(0)

    @pl.when(step == 0)
    def _():
        sums[...] = jnp.zeros_like(sums)

    x = data[...]
    y = targets[...]
    contract = (((0,), (0,)), ((), ()))

    def add(base, value):
        height, width = value.shape
        for k in range(width // LANES):
            rows = slice(base + k * height, base + (k + 1) * height)
            sums[rows, :] += value[:, k * LANES:(k + 1) * LANES]

    for j, (p, h) in enumerate(((p0, h0), (p1, h1), (p2, h2))):
        angle = jnp.dot(x, p[...], preferred_element_type=F32)
        turns = angle * TURN + h[0] * TURN
        f = scaled_cosine(turns, coefficients).astype(BF)
        held[j] = f
        feats[:, j * F:(j + 1) * F] = f
        add(MOMENT + 2 * F * j, lax.dot_general(f, y, contract, preferred_element_type=F32))
    left = held[index[3]]
    other = held[index[4]]
    add(GRAM, lax.dot_general(left, left, contract, preferred_element_type=F32))
    add(CROSS, lax.dot_general(left, other, contract, preferred_element_type=F32))


def features_call(index, data, projections, phases, targets):
    rows = data.shape[0]
    classes = targets.shape[1]
    kernel = functools.partial(features_kernel, sine_coefficients(math.sqrt(2.0 / F)))

    def columns(j):
        return pl.BlockSpec((data.shape[1], F), lambda i, n: (0, n[j]))

    def shift(j):
        return pl.BlockSpec((1, 1, F), lambda i, n: (n[j], 0, 0))

    return pl.pallas_call(
        kernel,
        grid_spec=pltpu.PrefetchScalarGridSpec(
            num_scalar_prefetch=1,
            grid=(rows // TILE,),
            in_specs=[
                pl.BlockSpec((TILE, data.shape[1]), lambda i, n: (i, 0)),
                *[columns(j) for j in range(NBLK)],
                *[shift(j) for j in range(NBLK)],
                pl.BlockSpec((TILE, classes), lambda i, n: (i, 0)),
            ],
            out_specs=[
                pl.BlockSpec((TILE, NBLK * F), lambda i, n: (i, 0)),
                pl.BlockSpec((HEIGHT, LANES), lambda i, n: (0, 0)),
            ],
            scratch_shapes=[pltpu.VMEM((NBLK, TILE, F), BF)],
        ),
        out_shape=[
            jax.ShapeDtypeStruct((rows, NBLK * F), BF),
            jax.ShapeDtypeStruct((HEIGHT, LANES), F32),
        ],
        name="features",
    )(index, data, *[projections] * 3, *[phases.reshape(NBLK, 1, F)] * 3, targets)


CHUNKS = ((GRAM, 4 * F), (CROSS, 4 * F), (MOMENT, 6 * F))
COPIES = 51


def mod4(v):
    return lax.rem(v + 8, 4)


class Place:
    def __init__(self):
        self.row = lax.axis_index("rows")
        self.plane = lax.axis_index("cls")
        self.core = lax.rem(self.row, 2)
        self.x = lax.rem(lax.div(self.row, 2), 4)
        self.y = lax.div(self.row, 8)
        self.partner = {"rows": self.row + 1 - 2 * self.core}

    def at(self, axis):
        return self.x if axis == "x" else self.y

    def near(self, axis, step):
        x = mod4(self.x + step) if axis == "x" else self.x
        y = mod4(self.y + step) if axis == "y" else self.y
        return {"rows": (y * 4 + x) * 2 + self.core}


def window(start, size):
    return pl.ds(pl.multiple_of(start, 8), size)


def reduce_chunk(place, q, base, height, v, out, r0, acc, ring1, ring2, part1, send_sem, recv_sem, copies):
    half = height // 2

    def send(k, source, target, device):
        copy = pltpu.make_async_remote_copy(
            src_ref=source, dst_ref=target, send_sem=send_sem.at[q, k], recv_sem=recv_sem.at[q, k],
            device_id=device, device_id_type=pl.DeviceIdType.MESH,
        )
        copy.start()
        copies.append(copy)
        return copy

    first = send(0, v.at[window(base + (1 - place.core) * half, half)], r0, place.partner)
    yield
    first.wait_recv()
    acc[...] = v[window(base + place.core * half, half), :] + r0[...]
    ways = [(part, h) for part in range(2) for h in range(2)]
    sign = (1, -1)

    def scatter(k, axes, source, origin, size, ring, store):
        small = size // 2

        def piece(part, i, h):
            return window(origin(part) + i * size + h * small, small)

        far, close, on = {}, {}, {}
        for part, h in ways:
            axis, s = axes[part], sign[h]
            i = place.at(axis)
            n = part * 2 + h
            far[n] = send(k + n, source.at[piece(part, mod4(i + 2), h)], ring.at[n, 0], place.near(axis, s))
            close[n] = send(k + 4 + n, source.at[piece(part, mod4(i - s), h)], ring.at[n, 1], place.near(axis, -s))
        yield
        for part, h in ways:
            axis, s = axes[part], sign[h]
            i = place.at(axis)
            n = part * 2 + h
            far[n].wait_recv()
            ring[n, 3] = source[piece(part, mod4(i + s), h), :] + ring[n, 0]
            on[n] = send(k + 8 + n, ring.at[n, 3], ring.at[n, 2], place.near(axis, s))
        yield
        for part, h in ways:
            i = place.at(axes[part])
            n = part * 2 + h
            close[n].wait_recv()
            on[n].wait_recv()
            store(part, h, source[piece(part, i, h), :] + ring[n, 1] + ring[n, 2])

    def gather(k, axes, origin, size):
        small = size // 2

        def piece(part, i, h):
            return out.at[window(base + origin(part) + i * size + h * small, small)]

        ahead, back, on = {}, {}, {}
        for part, h in ways:
            axis, s = axes[part], sign[h]
            n = part * 2 + h
            mine = piece(part, place.at(axis), h)
            ahead[n] = send(k + n, mine, mine, place.near(axis, s))
            back[n] = send(k + 4 + n, mine, mine, place.near(axis, -s))
        yield
        for part, h in ways:
            axis, s = axes[part], sign[h]
            n = part * 2 + h
            ahead[n].wait_recv()
            theirs = piece(part, mod4(place.at(axis) - s), h)
            on[n] = send(k + 8 + n, theirs, theirs, place.near(axis, s))
        yield
        for n in range(4):
            back[n].wait_recv()
            on[n].wait_recv()

    one, two = ("x", "y"), ("y", "x")
    quarter, sixteenth, last = height // 4, height // 16, height // 64

    def store1(part, h, value):
        part1[part * sixteenth + h * (sixteenth // 2):part * sixteenth + (h + 1) * (sixteenth // 2), :] = value

    yield from scatter(1, one, acc, lambda part: part * quarter, sixteenth, ring1, store1)

    def own(part):
        return place.core * half + part * quarter + place.at(one[part]) * sixteenth

    def store2(part, h, value):
        start = base + own(part) + place.at(two[part]) * last + h * (last // 2)
        out[window(start, last // 2), :] = value

    yield from scatter(13, two, part1, lambda part: part * sixteenth, last, ring2, store2)
    yield from gather(25, two, own, last)
    yield from gather(37, one, lambda part: place.core * half + part * quarter, sixteenth)
    finals = []
    for part in range(2):
        mine = out.at[window(base + place.core * half + part * quarter, quarter)]
        finals.append(send(49 + part, mine, mine, place.partner))
    yield
    for copy in finals:
        copy.wait_recv()


def exchange_kernel(scale, v, w_out, wh_out, out, s4, slabs, *scratch):
    place = Place()
    buffers, (send_sem, recv_sem, plane_send, plane_recv, wide_send, wide_recv) = scratch[:-6], scratch[-6:]
    me, plane = place.row, place.plane
    barrier = pltpu.get_barrier_semaphore()

    def greet(d, carry):
        pl.semaphore_signal(
            barrier, inc=1, device_id={"rows": lax.rem(me + d, ROWS)}, device_id_type=pl.DeviceIdType.MESH
        )
        return carry

    lax.fori_loop(1, ROWS, greet, 0)
    for d in range(1, PLANES):
        pl.semaphore_signal(
            barrier, inc=1, device_id={"cls": lax.rem(plane + d, PLANES)}, device_id_type=pl.DeviceIdType.MESH
        )
    pl.semaphore_wait(barrier, ROWS - 1 + PLANES - 1)

    copies = []
    runs = []
    for q, (base, height) in enumerate(CHUNKS):
        runs.append(reduce_chunk(place, q, base, height, v, out, *buffers[5 * q:5 * q + 5], send_sem, recv_sem, copies))
    done = [False] * len(runs)

    def advance(q):
        if not done[q]:
            try:
                next(runs[q])
            except StopIteration:
                done[q] = True

    lead = 0
    while not all(done[:2]):
        for q in range(min(lead + 1, len(runs))):
            advance(q)
        lead += 1

    def wide(base, width):
        return jnp.concatenate([out[base + k * F:base + (k + 1) * F, :] for k in range(width // LANES)], axis=1)

    eye = (
        lax.broadcasted_iota(jnp.int32, (F, F), 0) == lax.broadcasted_iota(jnp.int32, (F, F), 1)
    ).astype(F32)
    first = wide(GRAM, F) * scale[0] + eye * scale[1]
    part1 = split(first)
    second = scale[2] * (2.0 * first - dot3(part1, part1))
    advance(2)
    part2 = split(second)
    fourth = scale[3] * (2.0 * second - dot3(part2, part2))
    advance(2)
    part4 = split(fourth)
    s4[...] = fourth
    slab = s4[window(me * SLAB, SLAB), :]
    row = lax.broadcasted_iota(jnp.int32, (SLAB, F), 0) + me * SLAB
    column = lax.broadcasted_iota(jnp.int32, (SLAB, F), 1)
    unit = (row == column).astype(F32)
    eighth = scale[4] * (2.0 * slab - dot3(split(slab), part4))
    value = scale[5] * (2.0 * unit - eighth)
    value = scale[4] * (2.0 * value - dot3(split(value), part4))
    advance(2)
    value = scale[3] * (2.0 * value - dot3(split(value), part2))
    value = scale[2] * (2.0 * value - dot3(split(value), part1))
    value = value * scale[0]
    slabs[plane, 0] = value
    slabs[plane, 1] = dot3(split(value), split(wide(CROSS, F)))
    across = []
    for d in range(1, PLANES):
        copy = pltpu.make_async_remote_copy(
            src_ref=slabs.at[plane], dst_ref=slabs.at[plane], send_sem=plane_send.at[d], recv_sem=plane_recv.at[d],
            device_id={"cls": lax.rem(plane + d, PLANES)}, device_id_type=pl.DeviceIdType.MESH,
        )
        copy.start()
        across.append(copy)
    while not done[2]:
        advance(2)
    for copy in across:
        copy.wait_recv()

    def moment(j):
        return split(wide(MOMENT + 2 * F * j, 2 * LANES))

    def product(z, k, right):
        return dot3(split(slabs[z, k]), right)

    def product2(z, k, right):
        high, low = split(slabs[z, k])
        return jnp.dot(high, right, preferred_element_type=F32) + jnp.dot(low, right, preferred_element_type=F32)

    def broadcast(j, w):
        w_out[j] = w
        mine = wh_out.at[j, pl.ds(pl.multiple_of(me * SLAB, SLAB), SLAB)]
        wh_out[j, pl.ds(pl.multiple_of(me * SLAB, SLAB), SLAB), :] = w.astype(BF)

        def tell(d, carry):
            pltpu.make_async_remote_copy(
                src_ref=mine, dst_ref=mine, send_sem=wide_send.at[j], recv_sem=wide_recv.at[j],
                device_id={"rows": lax.rem(me + d, ROWS)}, device_id_type=pl.DeviceIdType.MESH,
            ).start()
            return carry

        lax.fori_loop(1, ROWS, tell, 0)

    def all_but_one(j):
        part = wh_out.at[j, pl.ds(0, (ROWS - 1) * SLAB)]
        return pltpu.make_async_remote_copy(
            src_ref=part, dst_ref=part, send_sem=wide_send.at[j], recv_sem=wide_recv.at[j],
            device_id=place.partner, device_id_type=pl.DeviceIdType.MESH,
        )

    broadcast(0, product(0, 0, moment(0)))
    w1 = product(1, 0, moment(1))
    w2 = product(2, 0, moment(2))
    all_but_one(0).wait_recv()
    broadcast(1, w1 - product2(1, 1, wh_out[0]))
    w2 = w2 - product2(2, 1, wh_out[0])
    all_but_one(1).wait_recv()
    broadcast(2, w2 - product2(3, 1, wh_out[1]))
    all_but_one(2).wait_recv()
    for copy in copies + across:
        copy.wait_send()
    for j in range(NBLK):
        all_but_one(j).wait_send()


def exchange_call(scale, sums, classes):
    vmem = pl.BlockSpec(memory_space=pltpu.VMEM)
    buffers = []
    for _, height in CHUNKS:
        buffers += [
            pltpu.VMEM((height // 2, LANES), F32),
            pltpu.VMEM((height // 2, LANES), F32),
            pltpu.VMEM((4, 4, height // 32, LANES), F32),
            pltpu.VMEM((4, 4, height // 128, LANES), F32),
            pltpu.VMEM((height // 8, LANES), F32),
        ]
    dma = pltpu.SemaphoreType.DMA
    return pl.pallas_call(
        exchange_kernel,
        in_specs=[pl.BlockSpec(memory_space=pltpu.SMEM), vmem],
        out_specs=[vmem, vmem],
        out_shape=[
            jax.ShapeDtypeStruct((NBLK, SLAB, classes), F32),
            jax.ShapeDtypeStruct((NBLK, F, classes), BF),
        ],
        scratch_shapes=[
            pltpu.VMEM((HEIGHT, LANES), F32),
            pltpu.VMEM((F, F), F32),
            pltpu.VMEM((PLANES, 2, SLAB, F), F32),
            *buffers,
            dma((len(CHUNKS), COPIES)),
            dma((len(CHUNKS), COPIES)),
            dma((PLANES,)),
            dma((PLANES,)),
            dma((NBLK,)),
            dma((NBLK,)),
        ],
        compiler_params=pltpu.CompilerParams(collective_id=0, has_side_effects=True),
        name="exchange",
    )(scale, sums)


def solve_scales(lower, upper, total):
    center = 0.5 * (upper + lower)
    u = 0.5 * (upper - lower) / center
    factors = []
    for _ in range(4):
        factors.append(2.0 / (2.0 - u * u))
        u = u * u / (2.0 - u * u)
    return jnp.stack([1.0 / (center * total), lower / center, *factors])


def body(data, projections, phases, targets, bounds, order):
    total = data.shape[0] * lax.axis_size("rows")
    plane = lax.axis_index("cls").astype(jnp.int32)
    left = jnp.minimum(plane, 2)
    other = jnp.maximum(plane - 2, 0)
    index = jnp.concatenate([order.astype(jnp.int32), left[None], other[None]])
    feats, sums = features_call(index, data, projections, phases, targets)
    bound = bounds[order[left]]
    scale = solve_scales(bound[0], bound[1], total)
    w, half = exchange_call(scale, sums, targets.shape[1])
    half = half.reshape(NBLK * F, -1)
    residual = targets.astype(F32) - jnp.dot(feats, half, preferred_element_type=F32)
    weights = jnp.zeros(w.shape, F32)
    for turn in range(NBLK):
        weights = lax.dynamic_update_slice(weights, w[turn][None], (order[turn], jnp.int32(0), jnp.int32(0)))
    return (weights, residual)


def solution(mesh):
    return jax.shard_map(
        body,
        mesh=mesh,
        in_specs=(P("rows", None), P(), P(), P("rows", "cls"), P(), P()),
        out_specs=(P(None, "rows", "cls"), P("rows", "cls")),
        check_vma=False,
    )
```

```python
import functools
import math

import jax
import jax.numpy as jnp
from jax import lax
from jax.experimental import pallas as pl
from jax.experimental.pallas import tpu as pltpu
from jax.sharding import PartitionSpec as P

F = 512
NBLK = 3
TILE = 512
RESIDUAL_TILE = 256
TILES = 4
SLAB = 16
BF = jnp.bfloat16
F32 = jnp.float32
LANES = 128
ROWS = 32
PLANES = 4
GRAM, CROSS, MOMENT, HEIGHT = 0, 4 * F, 8 * F, 14 * F
TURN = 1.0 / (2.0 * math.pi)


def sine_coefficients(scale):
    import numpy as np

    nodes = np.cos((np.arange(64) + 0.5) * math.pi / 64)
    u = (nodes + 1) / 2 / 16
    a = np.sqrt(u)
    fit = np.polynomial.polynomial.polyfit(u, np.sin(2 * math.pi * a) / a, 3, w=a)
    return [float(c) * scale for c in fit]


def scaled_cosine(turns, coefficients):
    a = 0.25 - jnp.abs(turns - jnp.round(turns))
    u = a * a
    value = coefficients[-1]
    for c in coefficients[-2::-1]:
        value = value * u + c
    return value * a


def split(x):
    high = x.astype(BF)
    return high, (x - high.astype(F32)).astype(BF)


def dot3(left, right, dims=(((1,), (0,)), ((), ()))):
    lh, ll = left
    rh, rl = right
    dot = functools.partial(lax.dot_general, dimension_numbers=dims, preferred_element_type=F32)
    return dot(lh, rh) + (dot(lh, rl) + dot(ll, rh))


def mod4(v):
    return lax.rem(v + 8, 4)


class Place:
    def __init__(self):
        self.row = lax.axis_index("rows")
        self.plane = lax.axis_index("cls")
        self.core = lax.rem(self.row, 2)
        self.x = lax.rem(lax.div(self.row, 2), 4)
        self.y = lax.div(self.row, 8)
        self.partner = {"rows": self.row + 1 - 2 * self.core}

    def at(self, axis):
        return self.x if axis == "x" else self.y

    def near(self, axis, step):
        x = mod4(self.x + step) if axis == "x" else self.x
        y = mod4(self.y + step) if axis == "y" else self.y
        return {"rows": (y * 4 + x) * 2 + self.core}


def window(start, size):
    return pl.ds(pl.multiple_of(start, 8), size)


CHUNKS = (
    (GRAM, 4 * F, (True, True, True, True)),
    (CROSS, 4 * F, (True, True, True, True)),
    (MOMENT, 6 * F, (False, True, True, False)),
)
COPIES = 51


def ring_shape(size, direct):
    return (2, 3, size, LANES) if direct else (4, 4, size // 2, LANES)


def reduce_chunk(place, q, v, out, r0, acc, ring1, ring2, part1, send_sem, recv_sem, copies):
    base, height, direct = CHUNKS[q]
    half = height // 2
    ways = [(part, h) for part in range(2) for h in range(2)]
    hops = [(part, d) for part in range(2) for d in range(1, 4)]
    sign = (1, -1)

    def send(k, source, target, device):
        copy = pltpu.make_async_remote_copy(
            src_ref=source, dst_ref=target, send_sem=send_sem.at[q, k], recv_sem=recv_sem.at[q, k],
            device_id=device, device_id_type=pl.DeviceIdType.MESH,
        )
        copy.start()
        copies.append(copy)
        return copy

    first = send(0, v.at[window(base + (1 - place.core) * half, half)], r0, place.partner)
    yield
    first.wait_recv()
    acc[...] = v[window(base + place.core * half, half), :] + r0[...]

    def scatter_direct(k, axes, source, origin, size, ring, store):
        flights = {}
        for part, d in sorted(hops, key=lambda hop: hop[1] != 2):
            target = mod4(place.at(axes[part]) + d)
            piece = source.at[window(origin(part) + target * size, size)]
            flights[part, d] = send(k + part * 3 + d - 1, piece, ring.at[part, d - 1], place.near(axes[part], d))
        yield
        for part in range(2):
            total = source[window(origin(part) + place.at(axes[part]) * size, size), :]
            for d in range(1, 4):
                flights[part, d].wait_recv()
                total = total + ring[part, d - 1]
            store(part, 0, total)

    def gather_direct(k, axes, origin, size):
        flights = []
        for part, d in sorted(hops, key=lambda hop: hop[1] != 2):
            mine = out.at[window(base + origin(part) + place.at(axes[part]) * size, size)]
            flights.append(send(k + part * 3 + d - 1, mine, mine, place.near(axes[part], d)))
        yield
        for copy in flights:
            copy.wait_recv()

    def scatter_ring(k, axes, source, origin, size, ring, store):
        small = size // 2

        def piece(part, i, h):
            return window(origin(part) + i * size + h * small, small)

        far, close, on = {}, {}, {}
        for part, h in ways:
            axis, s = axes[part], sign[h]
            i = place.at(axis)
            n = part * 2 + h
            far[n] = send(k + n, source.at[piece(part, mod4(i + 2), h)], ring.at[n, 0], place.near(axis, s))
            close[n] = send(k + 4 + n, source.at[piece(part, mod4(i - s), h)], ring.at[n, 1], place.near(axis, -s))
        yield
        for part, h in ways:
            axis, s = axes[part], sign[h]
            i = place.at(axis)
            n = part * 2 + h
            far[n].wait_recv()
            ring[n, 3] = source[piece(part, mod4(i + s), h), :] + ring[n, 0]
            on[n] = send(k + 8 + n, ring.at[n, 3], ring.at[n, 2], place.near(axis, s))
        yield
        for part, h in ways:
            i = place.at(axes[part])
            n = part * 2 + h
            close[n].wait_recv()
            on[n].wait_recv()
            store(part, h, source[piece(part, i, h), :] + ring[n, 1] + ring[n, 2])

    def gather_ring(k, axes, origin, size):
        small = size // 2

        def piece(part, i, h):
            return out.at[window(base + origin(part) + i * size + h * small, small)]

        ahead, back, on = {}, {}, {}
        for part, h in ways:
            axis, s = axes[part], sign[h]
            n = part * 2 + h
            mine = piece(part, place.at(axis), h)
            ahead[n] = send(k + n, mine, mine, place.near(axis, s))
            back[n] = send(k + 4 + n, mine, mine, place.near(axis, -s))
        yield
        for part, h in ways:
            axis, s = axes[part], sign[h]
            n = part * 2 + h
            ahead[n].wait_recv()
            theirs = piece(part, mod4(place.at(axis) - s), h)
            on[n] = send(k + 8 + n, theirs, theirs, place.near(axis, s))
        yield
        for n in range(4):
            back[n].wait_recv()
            on[n].wait_recv()

    def pick(straight, ringed, stage):
        return straight if direct[stage] else ringed

    one, two = ("x", "y"), ("y", "x")
    quarter, sixteenth, last = height // 4, height // 16, height // 64

    def store1(part, h, value):
        start = part * sixteenth + h * value.shape[0]
        part1[start:start + value.shape[0], :] = value

    scatter = pick(scatter_direct, scatter_ring, 0)
    yield from scatter(1, one, acc, lambda part: part * quarter, sixteenth, ring1, store1)

    def own(part):
        return place.core * half + part * quarter + place.at(one[part]) * sixteenth

    def store2(part, h, value):
        start = base + own(part) + place.at(two[part]) * last + h * value.shape[0]
        out[window(start, value.shape[0]), :] = value

    scatter = pick(scatter_direct, scatter_ring, 1)
    yield from scatter(13, two, part1, lambda part: part * sixteenth, last, ring2, store2)
    yield from pick(gather_direct, gather_ring, 2)(25, two, own, last)
    gather = pick(gather_direct, gather_ring, 3)
    yield from gather(37, one, lambda part: place.core * half + part * quarter, sixteenth)
    finals = []
    for part in range(2):
        mine = out.at[window(base + place.core * half + part * quarter, quarter)]
        finals.append(send(49 + part, mine, mine, place.partner))
    yield
    for copy in finals:
        copy.wait_recv()


def exchange_kernel(
    coefficients, order, bounds, phases, data_in, proj_in, targets_in, w_out, wh_out, feats_out,
    data, proj, chosen, targets, feats, v, out, s4, slabs, *scratch
):
    place = Place()
    buffers = scratch[:5 * len(CHUNKS)]
    send_sem, recv_sem, plane_send, plane_recv, wide_send, wide_recv, load_sem, store_sem = scratch[5 * len(CHUNKS):]
    me, plane = place.row, place.plane
    height = data.shape[0]
    loads = [pltpu.make_async_copy(proj_in, proj, load_sem.at[0])]
    for t in range(TILES):
        rows = pl.ds(t * TILE, TILE)
        loads.append(pltpu.make_async_copy(data_in.at[rows], data.at[rows], load_sem.at[1 + t]))
    loads.append(pltpu.make_async_copy(targets_in, targets, load_sem.at[1 + TILES]))
    for copy in loads:
        copy.start()

    barrier = pltpu.get_barrier_semaphore()

    def greet(d, carry):
        pl.semaphore_signal(
            barrier, inc=1, device_id={"rows": lax.rem(me + d, ROWS)}, device_id_type=pl.DeviceIdType.MESH
        )
        return carry

    lax.fori_loop(1, ROWS, greet, 0)
    for d in range(1, PLANES):
        pl.semaphore_signal(
            barrier, inc=1, device_id={"cls": lax.rem(plane + d, PLANES)}, device_id_type=pl.DeviceIdType.MESH
        )

    copies = []
    runs = [
        reduce_chunk(place, q, v, out, *buffers[5 * q:5 * q + 5], send_sem, recv_sem, copies)
        for q in range(len(CHUNKS))
    ]
    done = [False] * len(runs)

    def advance(*which):
        for q in which:
            if not done[q]:
                try:
                    next(runs[q])
                except StopIteration:
                    done[q] = True

    turn_a = jnp.minimum(plane, 2)
    turn_b = jnp.where(plane == 0, 1, jnp.where(plane == 3, 1, 0))
    turn_c = 3 - turn_a - turn_b
    contract = (((0,), (0,)), ((), ()))

    def pick(turn, values):
        block = order[turn]
        return jnp.where(block == 0, values[0], jnp.where(block == 1, values[1], values[2]))

    def columns(ref):
        return [ref[:, j * F:(j + 1) * F] for j in range(NBLK)]

    def choose(turn):
        chosen[...] = pick(turn, columns(proj))

    def features(turn, tiles):
        shift = pick(turn, columns(phases)) * TURN
        for t in tiles:
            rows = pl.ds(t * TILE, TILE)
            angle = jnp.dot(data[rows, :], chosen[...], preferred_element_type=F32)
            feats[turn, rows, :] = scaled_cosine(angle * TURN + shift, coefficients).astype(BF)

    def put(base, value):
        tall, width = value.shape
        for k in range(width // LANES):
            v[window(base + k * tall, tall), :] = value[:, k * LANES:(k + 1) * LANES]

    def keep(n, turn):
        copy = pltpu.make_async_copy(feats.at[turn], feats_out.at[turn], store_sem.at[n])
        copy.start()
        return copy

    def moments(turn):
        put(MOMENT + 2 * F * turn, lax.dot_general(feats[turn], targets[...], contract, preferred_element_type=F32))

    loads[0].wait()
    for t in range(TILES):
        loads[1 + t].wait()
    choose(turn_a)
    features(turn_a, range(TILES))
    put(GRAM, lax.dot_general(feats[turn_a], feats[turn_a], contract, preferred_element_type=F32))
    pl.semaphore_wait(barrier, ROWS - 1 + PLANES - 1)
    advance(0)
    choose(turn_b)
    features(turn_b, range(2))
    advance(0)
    features(turn_b, range(2, TILES))
    put(CROSS, lax.dot_general(feats[turn_a], feats[turn_b], contract, preferred_element_type=F32))
    advance(0, 1)
    choose(turn_c)
    features(turn_c, range(2))
    advance(0, 1)
    features(turn_c, range(2, TILES))
    advance(0)
    loads[1 + TILES].wait()
    for turn in (turn_a, turn_b, turn_c):
        moments(turn)
    advance(0, 1, 2)
    stores = [keep(n, turn) for n, turn in enumerate((turn_a, turn_b, turn_c))]
    while not done[0]:
        advance(0, 1, 2)

    def wide(base, width):
        return jnp.concatenate([out[window(base + k * F, F), :] for k in range(width // LANES)], axis=1)

    lower = jnp.full((1, F), pick(turn_a, [bounds[j, 0] for j in range(NBLK)]), F32)
    upper = jnp.full((1, F), pick(turn_a, [bounds[j, 1] for j in range(NBLK)]), F32)
    center = 0.5 * (upper + lower)
    u = 0.5 * (upper - lower) / center
    k1 = 2.0 / (2.0 - u * u)
    u = u * u / (2.0 - u * u)
    k2 = 2.0 / (2.0 - u * u)
    u = u * u / (2.0 - u * u)
    k4 = 2.0 / (2.0 - u * u)
    u = u * u / (2.0 - u * u)
    k8 = 2.0 / (2.0 - u * u)
    scale = 1.0 / (center * (height * ROWS))

    eye = (
        lax.broadcasted_iota(jnp.int32, (F, F), 0) == lax.broadcasted_iota(jnp.int32, (F, F), 1)
    ).astype(F32)
    first = wide(GRAM, F) * scale + eye * (lower / center)
    part1 = split(first)
    second = k1 * (2.0 * first - dot3(part1, part1))
    advance(1, 2)
    part2 = split(second)
    fourth = k2 * (2.0 * second - dot3(part2, part2))
    advance(1, 2)
    part4 = split(fourth)
    s4[...] = fourth
    slab = s4[window(me * SLAB, SLAB), :]
    row = lax.broadcasted_iota(jnp.int32, (SLAB, F), 0) + me * SLAB
    column = lax.broadcasted_iota(jnp.int32, (SLAB, F), 1)
    unit = (row == column).astype(F32)
    eighth = k4 * (2.0 * slab - dot3(split(slab), part4))
    value = k8 * (2.0 * unit - eighth)
    value = k4 * (2.0 * value - dot3(split(value), part4))
    value = k2 * (2.0 * value - dot3(split(value), part2))
    value = k1 * (2.0 * value - dot3(split(value), part1))
    value = value * scale
    across = [[], []]

    def cross_planes(k, value):
        slabs[plane, k] = value
        mine = slabs.at[plane, k]
        for d in range(1, PLANES):
            copy = pltpu.make_async_remote_copy(
                src_ref=mine, dst_ref=mine, send_sem=plane_send.at[k, d], recv_sem=plane_recv.at[k, d],
                device_id={"cls": lax.rem(plane + d, PLANES)}, device_id_type=pl.DeviceIdType.MESH,
            )
            copy.start()
            across[k].append(copy)

    cross_planes(0, value)
    while not done[1]:
        advance(1, 2)
    cross_planes(1, dot3(split(value), split(wide(CROSS, F))))
    while not done[2]:
        advance(2)

    def moment(j):
        return split(wide(MOMENT + 2 * F * j, 2 * LANES))

    def product(z, k, right):
        return dot3(split(slabs[z, k]), right)

    def product2(z, k, right):
        high, low = split(slabs[z, k])
        return jnp.dot(high, right, preferred_element_type=F32) + jnp.dot(low, right, preferred_element_type=F32)

    def broadcast(j, w):
        w_out[j] = w
        mine = wh_out.at[j, pl.ds(pl.multiple_of(me * SLAB, SLAB), SLAB)]
        wh_out[j, pl.ds(pl.multiple_of(me * SLAB, SLAB), SLAB), :] = w.astype(BF)

        def tell(d, carry):
            pltpu.make_async_remote_copy(
                src_ref=mine, dst_ref=mine, send_sem=wide_send.at[j], recv_sem=wide_recv.at[j],
                device_id={"rows": lax.rem(me + d, ROWS)}, device_id_type=pl.DeviceIdType.MESH,
            ).start()
            return carry

        lax.fori_loop(1, ROWS, tell, 0)

    def all_but_one(j):
        part = wh_out.at[j, pl.ds(0, (ROWS - 1) * SLAB)]
        return pltpu.make_async_remote_copy(
            src_ref=part, dst_ref=part, send_sem=wide_send.at[j], recv_sem=wide_recv.at[j],
            device_id=place.partner, device_id_type=pl.DeviceIdType.MESH,
        )

    for copy in across[0]:
        copy.wait_recv()
    broadcast(0, product(0, 0, moment(0)))
    w1 = product(1, 0, moment(1))
    w2 = product(2, 0, moment(2))
    for copy in across[1]:
        copy.wait_recv()
    all_but_one(0).wait_recv()
    broadcast(1, w1 - product2(1, 1, wh_out[0]))
    w2 = w2 - product2(2, 1, wh_out[0])
    all_but_one(1).wait_recv()
    broadcast(2, w2 - product2(3, 1, wh_out[1]))
    all_but_one(2).wait_recv()
    for copy in copies + across[0] + across[1]:
        copy.wait_send()
    for j in range(NBLK):
        all_but_one(j).wait_send()
    for copy in stores:
        copy.wait()


def exchange_call(order, bounds, phases, data, projections, targets):
    vmem = pl.BlockSpec(memory_space=pltpu.VMEM)
    smem = pl.BlockSpec(memory_space=pltpu.SMEM)
    hbm = pl.BlockSpec(memory_space=pl.ANY)
    rows, classes = targets.shape
    buffers = []
    for _, height, direct in CHUNKS:
        buffers += [
            pltpu.VMEM((height // 2, LANES), F32),
            pltpu.VMEM((height // 2, LANES), F32),
            pltpu.VMEM(ring_shape(height // 16, direct[0]), F32),
            pltpu.VMEM(ring_shape(height // 64, direct[1]), F32),
            pltpu.VMEM((height // 8, LANES), F32),
        ]
    dma = pltpu.SemaphoreType.DMA
    return pl.pallas_call(
        functools.partial(exchange_kernel, sine_coefficients(math.sqrt(2.0 / F))),
        in_specs=[smem, smem, vmem, hbm, hbm, hbm],
        out_specs=[vmem, vmem, hbm],
        out_shape=[
            jax.ShapeDtypeStruct((NBLK, SLAB, classes), F32),
            jax.ShapeDtypeStruct((NBLK, F, classes), BF),
            jax.ShapeDtypeStruct((NBLK, rows, F), BF),
        ],
        scratch_shapes=[
            pltpu.VMEM(data.shape, BF),
            pltpu.VMEM(projections.shape, BF),
            pltpu.VMEM((data.shape[1], F), BF),
            pltpu.VMEM(targets.shape, BF),
            pltpu.VMEM((NBLK, rows, F), BF),
            pltpu.VMEM((HEIGHT, LANES), F32),
            pltpu.VMEM((HEIGHT, LANES), F32),
            pltpu.VMEM((F, F), F32),
            pltpu.VMEM((PLANES, 2, SLAB, F), F32),
            *buffers,
            dma((len(CHUNKS), COPIES)),
            dma((len(CHUNKS), COPIES)),
            dma((2, PLANES)),
            dma((2, PLANES)),
            dma((NBLK,)),
            dma((NBLK,)),
            dma((2 + TILES,)),
            dma((NBLK,)),
        ],
        compiler_params=pltpu.CompilerParams(collective_id=0, has_side_effects=True),
        name="exchange",
    )(order, bounds, phases.reshape(1, -1), data, projections, targets)


def residual_kernel(order, feats, half, targets, w, weights, residual):
    @pl.when(pl.program_id(0) == 0)
    def _():
        for turn in range(NBLK):
            weights[order[turn]] = w[turn]

    total = jnp.dot(feats[0], half[0], preferred_element_type=F32)
    for turn in range(1, NBLK):
        total = total + jnp.dot(feats[turn], half[turn], preferred_element_type=F32)
    residual[...] = targets[...].astype(F32) - total


def residual_call(order, feats, half, targets, w):
    rows, classes = targets.shape
    tile = RESIDUAL_TILE
    return pl.pallas_call(
        residual_kernel,
        grid_spec=pltpu.PrefetchScalarGridSpec(
            num_scalar_prefetch=1,
            grid=(rows // tile,),
            in_specs=[
                pl.BlockSpec((NBLK, tile, F), lambda i, n: (0, i, 0)),
                pl.BlockSpec((NBLK, F, classes), lambda i, n: (0, 0, 0)),
                pl.BlockSpec((tile, classes), lambda i, n: (i, 0)),
                pl.BlockSpec((NBLK, SLAB, classes), lambda i, n: (0, 0, 0)),
            ],
            out_specs=[
                pl.BlockSpec((NBLK, SLAB, classes), lambda i, n: (0, 0, 0)),
                pl.BlockSpec((tile, classes), lambda i, n: (i, 0)),
            ],
        ),
        out_shape=[
            jax.ShapeDtypeStruct((NBLK, SLAB, classes), F32),
            jax.ShapeDtypeStruct((rows, classes), F32),
        ],
        name="residual",
    )(order, feats, half, targets, w)


def body(data, projections, phases, targets, bounds, order):
    w, half, feats = exchange_call(order, bounds, phases, data, projections, targets)
    weights, residual = residual_call(order, feats, half, targets, w)
    return (weights, residual)


def solution(mesh):
    return jax.shard_map(
        body,
        mesh=mesh,
        in_specs=(P("rows", None), P(), P(), P("rows", "cls"), P(), P()),
        out_specs=(P(None, "rows", "cls"), P("rows", "cls")),
        check_vma=False,
    )
```

```python
import functools
import math

import jax
import jax.numpy as jnp
from jax import lax
from jax.experimental import pallas as pl
from jax.experimental.pallas import tpu as pltpu
from jax.sharding import PartitionSpec as P

F = 512
NBLK = 3
TILE = 512
RESIDUAL_TILE = 512
TILES = 4
SLAB = 16
BF = jnp.bfloat16
F32 = jnp.float32
LANES = 128
ROWS = 32
PLANES = 4
GRAM, CROSS, MOMENT, HEIGHT = 0, 3 * F, 7 * F, 13 * F
HALF = F // 2
TURN = 1.0 / (2.0 * math.pi)


def sine_coefficients(scale):
    import numpy as np

    nodes = np.cos((np.arange(64) + 0.5) * math.pi / 64)
    u = (nodes + 1) / 2 / 16
    a = np.sqrt(u)
    fit = np.polynomial.polynomial.polyfit(u, np.sin(2 * math.pi * a) / a, 3, w=a)
    return [float(c) * scale for c in fit]


def scaled_cosine(turns, coefficients):
    a = 0.25 - jnp.abs(turns - jnp.round(turns))
    u = a * a
    value = coefficients[-1]
    for c in coefficients[-2::-1]:
        value = value * u + c
    return value * a


def split(x):
    high = x.astype(BF)
    return high, (x - high.astype(F32)).astype(BF)


def dot3(left, right, dims=(((1,), (0,)), ((), ()))):
    lh, ll = left
    rh, rl = right
    dot = functools.partial(lax.dot_general, dimension_numbers=dims, preferred_element_type=F32)
    return dot(lh, rh) + (dot(lh, rl) + dot(ll, rh))


def mod4(v):
    return lax.rem(v + 8, 4)


class Place:
    def __init__(self):
        self.row = lax.axis_index("rows")
        self.plane = lax.axis_index("cls")
        self.core = lax.rem(self.row, 2)
        self.x = lax.rem(lax.div(self.row, 2), 4)
        self.y = lax.div(self.row, 8)
        self.partner = {"rows": self.row + 1 - 2 * self.core}

    def at(self, axis):
        return self.x if axis == "x" else self.y

    def near(self, axis, step):
        x = mod4(self.x + step) if axis == "x" else self.x
        y = mod4(self.y + step) if axis == "y" else self.y
        return {"rows": (y * 4 + x) * 2 + self.core}


def window(start, size):
    return pl.ds(pl.multiple_of(start, 8), size)


CHUNKS = ((GRAM, 3 * F), (CROSS, 4 * F), (MOMENT, 2 * F), (MOMENT + 2 * F, 4 * F))
COPIES = 27


def reduce_chunk(place, q, v, out, r0, acc, ring1, ring2, part1, send_sem, recv_sem, copies):
    base, height = CHUNKS[q]
    half = height // 2
    hops = [(part, d) for d in (2, 1, 3) for part in range(2)]

    def send(k, source, target, device):
        copy = pltpu.make_async_remote_copy(
            src_ref=source, dst_ref=target, send_sem=send_sem.at[q, k], recv_sem=recv_sem.at[q, k],
            device_id=device, device_id_type=pl.DeviceIdType.MESH,
        )
        copy.start()
        copies.append(copy)
        return copy

    first = send(0, v.at[window(base + (1 - place.core) * half, half)], r0, place.partner)
    yield
    first.wait_recv()
    acc[...] = v[window(base + place.core * half, half), :] + r0[...]

    def scatter(k, axes, source, origin, size, ring, store):
        flights = {}
        for part, d in hops:
            target = mod4(place.at(axes[part]) + d)
            piece = source.at[window(origin(part) + target * size, size)]
            flights[part, d] = send(k + part * 3 + d - 1, piece, ring.at[part, d - 1], place.near(axes[part], d))
        yield
        for part in range(2):
            total = source[window(origin(part) + place.at(axes[part]) * size, size), :]
            for d in range(1, 4):
                flights[part, d].wait_recv()
                total = total + ring[part, d - 1]
            store(part, total)

    def gather(k, axes, origin, size):
        flights = []
        for part, d in hops:
            mine = out.at[window(base + origin(part) + place.at(axes[part]) * size, size)]
            flights.append(send(k + part * 3 + d - 1, mine, mine, place.near(axes[part], d)))
        yield
        for copy in flights:
            copy.wait_recv()

    one, two = ("x", "y"), ("y", "x")
    quarter, sixteenth, last = height // 4, height // 16, height // 64

    def store1(part, value):
        part1[part * sixteenth:(part + 1) * sixteenth, :] = value

    yield from scatter(1, one, acc, lambda part: part * quarter, sixteenth, ring1, store1)

    def own(part):
        return place.core * half + part * quarter + place.at(one[part]) * sixteenth

    def store2(part, value):
        out[window(base + own(part) + place.at(two[part]) * last, last), :] = value

    yield from scatter(7, two, part1, lambda part: part * sixteenth, last, ring2, store2)
    yield from gather(13, two, own, last)
    yield from gather(19, one, lambda part: place.core * half + part * quarter, sixteenth)
    finals = []
    for part in range(2):
        mine = out.at[window(base + place.core * half + part * quarter, quarter)]
        finals.append(send(25 + part, mine, mine, place.partner))
    yield
    for copy in finals:
        copy.wait_recv()


def exchange_kernel(
    coefficients, order, bounds, phases, data_in, proj_in, targets_in, w_out, wh_out, feats_out, left_out,
    data, proj, chosen, targets, feats, left, v, out, s4, slabs, *scratch
):
    place = Place()
    buffers = scratch[:5 * len(CHUNKS)]
    send_sem, recv_sem, plane_send, plane_recv, wide_send, wide_recv, load_sem, store_sem = scratch[5 * len(CHUNKS):]
    me, plane = place.row, place.plane
    height = data.shape[0]
    loads = [pltpu.make_async_copy(proj_in, proj, load_sem.at[0])]
    for t in range(TILES):
        rows = pl.ds(t * TILE, TILE)
        loads.append(pltpu.make_async_copy(data_in.at[rows], data.at[rows], load_sem.at[1 + t]))
    loads.append(pltpu.make_async_copy(targets_in, targets, load_sem.at[1 + TILES]))
    for copy in loads:
        copy.start()

    barrier = pltpu.get_barrier_semaphore()

    def greet(d, carry):
        pl.semaphore_signal(
            barrier, inc=1, device_id={"rows": lax.rem(me + d, ROWS)}, device_id_type=pl.DeviceIdType.MESH
        )
        return carry

    lax.fori_loop(1, ROWS, greet, 0)
    for d in range(1, PLANES):
        pl.semaphore_signal(
            barrier, inc=1, device_id={"cls": lax.rem(plane + d, PLANES)}, device_id_type=pl.DeviceIdType.MESH
        )

    copies = []
    runs = [
        reduce_chunk(place, q, v, out, *buffers[5 * q:5 * q + 5], send_sem, recv_sem, copies)
        for q in range(len(CHUNKS))
    ]
    done = [False] * len(runs)

    def advance(*which):
        for q in which:
            if not done[q]:
                try:
                    next(runs[q])
                except StopIteration:
                    done[q] = True

    turn_a = jnp.minimum(plane, 2)
    turn_b = jnp.where(plane == 0, 1, jnp.where(plane == 3, 1, 0))
    turn_c = 3 - turn_a - turn_b
    contract = (((0,), (0,)), ((), ()))

    def pick(turn, values):
        block = order[turn]
        return jnp.where(block == 0, values[0], jnp.where(block == 1, values[1], values[2]))

    def columns(ref):
        return [ref[:, j * F:(j + 1) * F] for j in range(NBLK)]

    def choose(turn):
        chosen[...] = pick(turn, columns(proj))

    def features(turn, tiles):
        shift = pick(turn, [phases[j * F:(j + 1) * F] for j in range(NBLK)])[None, :] * TURN
        for t in tiles:
            rows = pl.ds(t * TILE, TILE)
            angle = jnp.dot(data[rows, :], chosen[...], preferred_element_type=F32)
            feats[turn, rows, :] = scaled_cosine(angle * TURN + shift, coefficients).astype(BF)

    def put(base, value):
        tall, width = value.shape
        for k in range(width // LANES):
            v[window(base + k * tall, tall), :] = value[:, k * LANES:(k + 1) * LANES]

    def moments(turn):
        put(MOMENT + 2 * F * turn, lax.dot_general(feats[turn], targets[...], contract, preferred_element_type=F32))

    def gram():
        for n in range(2):
            lhs = feats[turn_a, :, n * HALF:(n + 1) * HALF]
            rhs = feats[turn_a, :, n * HALF:]
            put(GRAM + n * 2 * F, lax.dot_general(lhs, rhs, contract, preferred_element_type=F32))

    G, C, M, N = range(4)
    loads[0].wait()
    choose(turn_a)
    for t in range(TILES):
        loads[1 + t].wait()
        features(turn_a, [t])
    gram()
    pl.semaphore_wait(barrier, ROWS - 1 + PLANES - 1)
    advance(G)
    choose(turn_b)
    features(turn_b, range(2))
    advance(G)
    features(turn_b, range(2, TILES))
    put(CROSS, lax.dot_general(feats[turn_a], feats[turn_b], contract, preferred_element_type=F32))
    advance(C)
    choose(turn_c)
    features(turn_c, range(3))
    advance(G, C)
    features(turn_c, range(3, TILES))
    loads[1 + TILES].wait()
    moments(0)
    advance(M)
    moments(1)
    moments(2)
    keep = pltpu.make_async_copy(feats.at[NBLK - 1], feats_out, store_sem.at[0])
    keep.start()
    advance(G, N, M, N, C, G, M, N, C, G, M, N, C, G)

    def wide(base, width, tall=F):
        return jnp.concatenate([out[window(base + k * tall, tall), :] for k in range(width // LANES)], axis=1)

    lower = jnp.full((1, F), pick(turn_a, [bounds[0, j] for j in range(NBLK)]), F32)
    upper = jnp.full((1, F), pick(turn_a, [bounds[1, j] for j in range(NBLK)]), F32)
    center = 0.5 * (upper + lower)
    u = 0.5 * (upper - lower) / center
    k1 = 2.0 / (2.0 - u * u)
    u = u * u / (2.0 - u * u)
    k2 = 2.0 / (2.0 - u * u)
    u = u * u / (2.0 - u * u)
    k4 = 2.0 / (2.0 - u * u)
    u = u * u / (2.0 - u * u)
    k8 = 2.0 / (2.0 - u * u)
    scale = 1.0 / (center * (height * ROWS))

    eye = (
        lax.broadcasted_iota(jnp.int32, (F, F), 0) == lax.broadcasted_iota(jnp.int32, (F, F), 1)
    ).astype(F32)
    top = wide(GRAM, F, HALF)
    corner = wide(GRAM + 2 * F, HALF, HALF)
    whole = jnp.concatenate([top, jnp.concatenate([top[:, HALF:].T, corner], axis=1)], axis=0)
    first = whole * scale + eye * (lower / center)
    part1 = split(first)
    second = k1 * (2.0 * first - dot3(part1, part1))
    part2 = split(second)
    fourth = k2 * (2.0 * second - dot3(part2, part2))
    advance(M, N)
    part4 = split(fourth)
    s4[...] = fourth
    slab = s4[window(me * SLAB, SLAB), :]
    row = lax.broadcasted_iota(jnp.int32, (SLAB, F), 0) + me * SLAB
    column = lax.broadcasted_iota(jnp.int32, (SLAB, F), 1)
    unit = (row == column).astype(F32)
    eighth = k4 * (2.0 * slab - dot3(split(slab), part4))
    value = k8 * (2.0 * unit - eighth)
    value = k4 * (2.0 * value - dot3(split(value), part4))
    value = k2 * (2.0 * value - dot3(split(value), part2))
    value = k1 * (2.0 * value - dot3(split(value), part1))
    value = value * scale
    across = [[], []]

    def cross_planes(k, value):
        slabs[plane, k] = value
        mine = slabs.at[plane, k]
        for d in range(1, PLANES):
            copy = pltpu.make_async_remote_copy(
                src_ref=mine, dst_ref=mine, send_sem=plane_send.at[k, d], recv_sem=plane_recv.at[k, d],
                device_id={"cls": lax.rem(plane + d, PLANES)}, device_id_type=pl.DeviceIdType.MESH,
            )
            copy.start()
            across[k].append(copy)

    cross_planes(0, value)
    advance(C, M, C)
    cross_planes(1, dot3(split(value), split(wide(CROSS, F))))
    advance(M)

    def moment(j):
        return split(wide(MOMENT + 2 * F * j, 2 * LANES))

    def product(z, k, right):
        return dot3(split(slabs[z, k]), right)

    def product2(z, k, right):
        high, low = split(slabs[z, k])
        return jnp.dot(high, right, preferred_element_type=F32) + jnp.dot(low, right, preferred_element_type=F32)

    def broadcast(j, w):
        w_out[j] = w
        mine = wh_out.at[j, pl.ds(pl.multiple_of(me * SLAB, SLAB), SLAB)]
        wh_out[j, pl.ds(pl.multiple_of(me * SLAB, SLAB), SLAB), :] = w.astype(BF)

        def tell(d, carry):
            pltpu.make_async_remote_copy(
                src_ref=mine, dst_ref=mine, send_sem=wide_send.at[j], recv_sem=wide_recv.at[j],
                device_id={"rows": lax.rem(me + d, ROWS)}, device_id_type=pl.DeviceIdType.MESH,
            ).start()
            return carry

        lax.fori_loop(1, ROWS, tell, 0)

    def all_but_one(j):
        part = wh_out.at[j, pl.ds(0, (ROWS - 1) * SLAB)]
        return pltpu.make_async_remote_copy(
            src_ref=part, dst_ref=part, send_sem=wide_send.at[j], recv_sem=wide_recv.at[j],
            device_id=place.partner, device_id_type=pl.DeviceIdType.MESH,
        )

    def subtract(turn, start):
        for t in range(TILES):
            rows = pl.ds(t * TILE, TILE)
            before = targets[rows, :].astype(F32) if start else left[rows, :]
            left[rows, :] = before - jnp.dot(feats[turn, rows, :], wh_out[turn], preferred_element_type=F32)

    for copy in across[0]:
        copy.wait_recv()
    broadcast(0, product(0, 0, moment(0)))
    advance(N, N)
    assert all(done)
    w1 = product(1, 0, moment(1))
    w2 = product(2, 0, moment(2))
    for copy in across[1]:
        copy.wait_recv()
    all_but_one(0).wait_recv()
    broadcast(1, w1 - product2(1, 1, wh_out[0]))
    w2 = w2 - product2(2, 1, wh_out[0])
    subtract(0, True)
    all_but_one(1).wait_recv()
    broadcast(2, w2 - product2(3, 1, wh_out[1]))
    subtract(1, False)
    hand = pltpu.make_async_copy(left, left_out, store_sem.at[1])
    hand.start()
    all_but_one(2).wait_recv()
    for copy in copies + across[0] + across[1]:
        copy.wait_send()
    for j in range(NBLK):
        all_but_one(j).wait_send()
    keep.wait()
    hand.wait()


def exchange_call(order, bounds, phases, data, projections, targets):
    vmem = pl.BlockSpec(memory_space=pltpu.VMEM)
    smem = pl.BlockSpec(memory_space=pltpu.SMEM)
    hbm = pl.BlockSpec(memory_space=pl.ANY)
    rows, classes = targets.shape
    buffers = []
    for _, height in CHUNKS:
        buffers += [
            pltpu.VMEM((height // 2, LANES), F32),
            pltpu.VMEM((height // 2, LANES), F32),
            pltpu.VMEM((2, 3, height // 16, LANES), F32),
            pltpu.VMEM((2, 3, height // 64, LANES), F32),
            pltpu.VMEM((height // 8, LANES), F32),
        ]
    dma = pltpu.SemaphoreType.DMA
    return pl.pallas_call(
        functools.partial(exchange_kernel, sine_coefficients(math.sqrt(2.0 / F))),
        in_specs=[smem, smem, vmem, hbm, hbm, hbm],
        out_specs=[vmem, vmem, hbm, hbm],
        out_shape=[
            jax.ShapeDtypeStruct((NBLK, SLAB, classes), F32),
            jax.ShapeDtypeStruct((NBLK, F, classes), BF),
            jax.ShapeDtypeStruct((rows, F), BF),
            jax.ShapeDtypeStruct((rows, classes), F32),
        ],
        scratch_shapes=[
            pltpu.VMEM(data.shape, BF),
            pltpu.VMEM(projections.shape, BF),
            pltpu.VMEM((data.shape[1], F), BF),
            pltpu.VMEM(targets.shape, BF),
            pltpu.VMEM((NBLK, rows, F), BF),
            pltpu.VMEM((rows, classes), F32),
            pltpu.VMEM((HEIGHT, LANES), F32),
            pltpu.VMEM((HEIGHT, LANES), F32),
            pltpu.VMEM((F, F), F32),
            pltpu.VMEM((PLANES, 2, SLAB, F), F32),
            *buffers,
            dma((len(CHUNKS), COPIES)),
            dma((len(CHUNKS), COPIES)),
            dma((2, PLANES)),
            dma((2, PLANES)),
            dma((NBLK,)),
            dma((NBLK,)),
            dma((2 + TILES,)),
            dma((2,)),
        ],
        compiler_params=pltpu.CompilerParams(collective_id=0, has_side_effects=True),
        name="exchange",
    )(order, bounds.T, phases, data, projections, targets)


def residual_kernel(order, feats, half, left, w, weights, residual):
    @pl.when(pl.program_id(0) == 0)
    def _():
        for turn in range(NBLK):
            weights[order[turn]] = w[turn]

    residual[...] = left[...] - jnp.dot(feats[...], half[0], preferred_element_type=F32)


def residual_call(order, feats, half, left, w):
    rows, classes = left.shape
    tile = RESIDUAL_TILE
    return pl.pallas_call(
        residual_kernel,
        grid_spec=pltpu.PrefetchScalarGridSpec(
            num_scalar_prefetch=1,
            grid=(rows // tile,),
            in_specs=[
                pl.BlockSpec((tile, F), lambda i, n: (i, 0)),
                pl.BlockSpec((1, F, classes), lambda i, n: (NBLK - 1, 0, 0)),
                pl.BlockSpec((tile, classes), lambda i, n: (i, 0)),
                pl.BlockSpec((NBLK, SLAB, classes), lambda i, n: (0, 0, 0)),
            ],
            out_specs=[
                pl.BlockSpec((NBLK, SLAB, classes), lambda i, n: (0, 0, 0)),
                pl.BlockSpec((tile, classes), lambda i, n: (i, 0)),
            ],
        ),
        out_shape=[
            jax.ShapeDtypeStruct((NBLK, SLAB, classes), F32),
            jax.ShapeDtypeStruct((rows, classes), F32),
        ],
        name="residual",
    )(order, feats, half, left, w)


def body(data, projections, phases, targets, bounds, order):
    w, half, feats, left = exchange_call(order, bounds, phases, data, projections, targets)
    weights, residual = residual_call(order, feats, half, left, w)
    return (weights, residual)


def solution(mesh):
    return jax.shard_map(
        body,
        mesh=mesh,
        in_specs=(P("rows", None), P(), P(), P("rows", "cls"), P(), P()),
        out_specs=(P(None, "rows", "cls"), P("rows", "cls")),
        check_vma=False,
    )
```

```python
import functools
import math

import jax
import jax.numpy as jnp
from jax import lax
from jax.experimental import pallas as pl
from jax.experimental.pallas import tpu as pltpu
from jax.sharding import PartitionSpec as P

F = 512
NBLK = 3
TILE = 512
RESIDUAL_TILE = 512
TILES = 4
SLAB = 16
BF = jnp.bfloat16
F32 = jnp.float32
LANES = 128
ROWS = 32
PLANES = 4
GRAM, CROSS, MOMENT, HEIGHT = 0, 3 * F, 7 * F, 13 * F
HALF = F // 2
TURN = 1.0 / (2.0 * math.pi)


def sine_coefficients(scale):
    import numpy as np

    nodes = np.cos((np.arange(64) + 0.5) * math.pi / 64)
    u = (nodes + 1) / 2 / 16
    a = np.sqrt(u)
    fit = np.polynomial.polynomial.polyfit(u, np.sin(2 * math.pi * a) / a, 3, w=a)
    return [float(c) * scale for c in fit]


def scaled_cosine(turns, coefficients):
    a = 0.25 - jnp.abs(turns - jnp.round(turns))
    u = a * a
    value = coefficients[-1]
    for c in coefficients[-2::-1]:
        value = value * u + c
    return value * a


def split(x):
    high = x.astype(BF)
    return high, (x - high.astype(F32)).astype(BF)


def dot3(left, right, dims=(((1,), (0,)), ((), ()))):
    lh, ll = left
    rh, rl = right
    dot = functools.partial(lax.dot_general, dimension_numbers=dims, preferred_element_type=F32)
    return dot(lh, rh) + (dot(lh, rl) + dot(ll, rh))


def mod4(v):
    return lax.rem(v + 8, 4)


class Place:
    def __init__(self):
        self.row = lax.axis_index("rows")
        self.plane = lax.axis_index("cls")
        self.core = lax.rem(self.row, 2)
        self.x = lax.rem(lax.div(self.row, 2), 4)
        self.y = lax.div(self.row, 8)
        self.partner = {"rows": self.row + 1 - 2 * self.core}

    def at(self, axis):
        return self.x if axis == "x" else self.y

    def near(self, axis, step):
        x = mod4(self.x + step) if axis == "x" else self.x
        y = mod4(self.y + step) if axis == "y" else self.y
        return {"rows": (y * 4 + x) * 2 + self.core}


def window(start, size):
    return pl.ds(pl.multiple_of(start, 8), size)


CHUNKS = ((GRAM, 3 * F), (CROSS, 4 * F), (MOMENT, 2 * F), (MOMENT + 2 * F, 4 * F))
COPIES = 27


def reduce_chunk(place, q, v, out, r0, acc, ring1, ring2, part1, send_sem, recv_sem, copies):
    base, height = CHUNKS[q]
    half = height // 2
    hops = [(part, d) for d in (2, 1, 3) for part in range(2)]

    def send(k, source, target, device):
        copy = pltpu.make_async_remote_copy(
            src_ref=source, dst_ref=target, send_sem=send_sem.at[q, k], recv_sem=recv_sem.at[q, k],
            device_id=device, device_id_type=pl.DeviceIdType.MESH,
        )
        copy.start()
        copies.append(copy)
        return copy

    first = send(0, v.at[window(base + (1 - place.core) * half, half)], r0, place.partner)
    yield
    first.wait_recv()
    acc[...] = v[window(base + place.core * half, half), :] + r0[...]

    def scatter(k, axes, source, origin, size, ring, store):
        flights = {}
        for part, d in hops:
            target = mod4(place.at(axes[part]) + d)
            piece = source.at[window(origin(part) + target * size, size)]
            flights[part, d] = send(k + part * 3 + d - 1, piece, ring.at[part, d - 1], place.near(axes[part], d))
        yield
        for part in range(2):
            total = source[window(origin(part) + place.at(axes[part]) * size, size), :]
            for d in range(1, 4):
                flights[part, d].wait_recv()
                total = total + ring[part, d - 1]
            store(part, total)

    def gather(k, axes, origin, size):
        flights = []
        for part, d in hops:
            mine = out.at[window(base + origin(part) + place.at(axes[part]) * size, size)]
            flights.append(send(k + part * 3 + d - 1, mine, mine, place.near(axes[part], d)))
        yield
        for copy in flights:
            copy.wait_recv()

    one, two = ("x", "y"), ("y", "x")
    quarter, sixteenth, last = height // 4, height // 16, height // 64

    def store1(part, value):
        part1[part * sixteenth:(part + 1) * sixteenth, :] = value

    yield from scatter(1, one, acc, lambda part: part * quarter, sixteenth, ring1, store1)

    def own(part):
        return place.core * half + part * quarter + place.at(one[part]) * sixteenth

    def store2(part, value):
        out[window(base + own(part) + place.at(two[part]) * last, last), :] = value

    yield from scatter(7, two, part1, lambda part: part * sixteenth, last, ring2, store2)
    yield from gather(13, two, own, last)
    yield from gather(19, one, lambda part: place.core * half + part * quarter, sixteenth)
    finals = []
    for part in range(2):
        mine = out.at[window(base + place.core * half + part * quarter, quarter)]
        finals.append(send(25 + part, mine, mine, place.partner))
    yield
    for copy in finals:
        copy.wait_recv()


def exchange_kernel(
    coefficients, order, bounds, phases, data_in, proj_in, targets_in, w_out, wh_out, feats_out, left_out,
    data, proj, chosen, targets, feats, left, v, out, s1, slabs, *scratch
):
    place = Place()
    buffers = scratch[:5 * len(CHUNKS)]
    send_sem, recv_sem, plane_send, plane_recv, wide_send, wide_recv, load_sem, store_sem = scratch[5 * len(CHUNKS):]
    me, plane = place.row, place.plane
    height = data.shape[0]
    loads = [pltpu.make_async_copy(proj_in, proj, load_sem.at[0])]
    for t in range(TILES):
        rows = pl.ds(t * TILE, TILE)
        loads.append(pltpu.make_async_copy(data_in.at[rows], data.at[rows], load_sem.at[1 + t]))
    loads.append(pltpu.make_async_copy(targets_in, targets, load_sem.at[1 + TILES]))
    for copy in loads:
        copy.start()

    barrier = pltpu.get_barrier_semaphore()

    greeted = [place.partner]
    greeted += [place.near(axis, d) for axis in ("x", "y") for d in range(1, 4)]
    greeted += [{"cls": lax.rem(plane + d, PLANES)} for d in range(1, PLANES)]
    for device in greeted:
        pl.semaphore_signal(barrier, inc=1, device_id=device, device_id_type=pl.DeviceIdType.MESH)

    copies = []
    runs = [
        reduce_chunk(place, q, v, out, *buffers[5 * q:5 * q + 5], send_sem, recv_sem, copies)
        for q in range(len(CHUNKS))
    ]
    done = [False] * len(runs)

    def advance(*which):
        for q in which:
            if not done[q]:
                try:
                    next(runs[q])
                except StopIteration:
                    done[q] = True

    turn_a = jnp.minimum(plane, 2)
    turn_b = jnp.where(plane == 0, 1, 0)
    turn_c = 3 - turn_a - turn_b
    turn_x = jnp.where(plane == 3, 1, 0)
    contract = (((0,), (0,)), ((), ()))

    def pick(turn, values):
        block = order[turn]
        return jnp.where(block == 0, values[0], jnp.where(block == 1, values[1], values[2]))

    def columns(ref):
        return [ref[:, j * F:(j + 1) * F] for j in range(NBLK)]

    def choose(turn):
        chosen[...] = pick(turn, columns(proj))

    def features(turn, tiles):
        shift = pick(turn, [phases[j * F:(j + 1) * F] for j in range(NBLK)])[None, :] * TURN
        for t in tiles:
            rows = pl.ds(t * TILE, TILE)
            angle = jnp.dot(data[rows, :], chosen[...], preferred_element_type=F32)
            feats[turn, rows, :] = scaled_cosine(angle * TURN + shift, coefficients).astype(BF)

    def put(base, value):
        tall, width = value.shape
        for k in range(width // LANES):
            v[window(base + k * tall, tall), :] = value[:, k * LANES:(k + 1) * LANES]

    def moments(turn):
        put(MOMENT + 2 * F * turn, lax.dot_general(feats[turn], targets[...], contract, preferred_element_type=F32))

    def gram():
        for n in range(2):
            lhs = feats[turn_a, :, n * HALF:(n + 1) * HALF]
            rhs = feats[turn_a, :, n * HALF:]
            put(GRAM + n * 2 * F, lax.dot_general(lhs, rhs, contract, preferred_element_type=F32))

    G, C, M, N = range(4)
    loads[0].wait()
    choose(turn_a)
    for t in range(TILES):
        loads[1 + t].wait()
        features(turn_a, [t])
    gram()
    pl.semaphore_wait(barrier, len(greeted))
    advance(G)
    choose(turn_b)
    features(turn_b, range(3))
    advance(G)
    features(turn_b, range(3, TILES))
    loads[1 + TILES].wait()
    moments(0)
    choose(turn_c)
    features(turn_c, range(2))
    advance(M)
    features(turn_c, range(2, TILES))
    advance(G)
    put(CROSS, lax.dot_general(feats[turn_a], feats[turn_x], contract, preferred_element_type=F32))
    advance(C, M)
    moments(1)
    moments(2)
    keep = pltpu.make_async_copy(feats.at[NBLK - 1], feats_out, store_sem.at[0])
    keep.start()
    advance(G, C, N, M, N, G, C, M, N, G, C, M, N, C, G)

    def wide(base, width, tall=F):
        return jnp.concatenate([out[window(base + k * tall, tall), :] for k in range(width // LANES)], axis=1)

    lower = jnp.full((1, F), pick(turn_a, [bounds[0, j] for j in range(NBLK)]), F32)
    upper = jnp.full((1, F), pick(turn_a, [bounds[1, j] for j in range(NBLK)]), F32)
    center = 0.5 * (upper + lower)
    u = 0.5 * (upper - lower) / center
    k1 = 2.0 / (2.0 - u * u)
    u = u * u / (2.0 - u * u)
    k2 = 2.0 / (2.0 - u * u)
    u = u * u / (2.0 - u * u)
    k4 = 2.0 / (2.0 - u * u)
    u = u * u / (2.0 - u * u)
    k8 = 2.0 / (2.0 - u * u)
    scale = 1.0 / (center * (height * ROWS))

    eye = (
        lax.broadcasted_iota(jnp.int32, (F, F), 0) == lax.broadcasted_iota(jnp.int32, (F, F), 1)
    ).astype(F32)
    top = wide(GRAM, F, HALF)
    corner = wide(GRAM + 2 * F, HALF, HALF)
    whole = jnp.concatenate([top, jnp.concatenate([top[:, HALF:].T, corner], axis=1)], axis=0)
    first = whole * scale + eye * (lower / center)
    s1[...] = first
    row = lax.broadcasted_iota(jnp.int32, (SLAB, F), 0) + me * SLAB
    column = lax.broadcasted_iota(jnp.int32, (SLAB, F), 1)
    unit = (row == column).astype(F32)
    value = k1 * (2.0 * unit - s1[window(me * SLAB, SLAB), :])
    part1 = split(first)
    second = k1 * (2.0 * first - dot3(part1, part1))
    advance(M)
    part2 = split(second)
    value = k2 * (2.0 * value - dot3(split(value), part2))
    fourth = k2 * (2.0 * second - dot3(part2, part2))
    advance(N)
    part4 = split(fourth)
    value = k4 * (2.0 * value - dot3(split(value), part4))
    once = dot3(split(value), part4)
    value = k8 * (2.0 * value - k4 * (2.0 * once - dot3(split(once), part4)))
    value = value * scale
    sends = (plane != PLANES - 1, plane != 0)

    def slab_copy(k, source, d):
        return pltpu.make_async_remote_copy(
            src_ref=slabs.at[source, k], dst_ref=slabs.at[source, k],
            send_sem=plane_send.at[k, d], recv_sem=plane_recv.at[k, source],
            device_id={"cls": lax.rem(plane + d, PLANES)}, device_id_type=pl.DeviceIdType.MESH,
        )

    def cross_planes(k, value):
        slabs[plane, k] = value

        @pl.when(sends[k])
        def _():
            for d in (2, 1, 3):
                slab_copy(k, plane, d).start()

    def arrived(k, source):
        @pl.when(plane != source)
        def _():
            slab_copy(k, source, 1).wait_recv()

    cross_planes(0, value)
    advance(M, C, C)
    cross_planes(1, dot3(split(value), split(wide(CROSS, F))))

    def moment(j):
        return split(wide(MOMENT + 2 * F * j, 2 * LANES))

    def product(z, k, right):
        return dot3(split(slabs[z, k]), right)

    def product2(z, k, right):
        high, low = split(slabs[z, k])
        return jnp.dot(high, right, preferred_element_type=F32) + jnp.dot(low, right, preferred_element_type=F32)

    def broadcast(j, w):
        w_out[j] = w
        mine = wh_out.at[j, pl.ds(pl.multiple_of(me * SLAB, SLAB), SLAB)]
        wh_out[j, pl.ds(pl.multiple_of(me * SLAB, SLAB), SLAB), :] = w.astype(BF)

        def tell(d, carry):
            pltpu.make_async_remote_copy(
                src_ref=mine, dst_ref=mine, send_sem=wide_send.at[j], recv_sem=wide_recv.at[j],
                device_id={"rows": lax.rem(me + d, ROWS)}, device_id_type=pl.DeviceIdType.MESH,
            ).start()
            return carry

        lax.fori_loop(1, ROWS, tell, 0)

    def all_but_one(j):
        part = wh_out.at[j, pl.ds(0, (ROWS - 1) * SLAB)]
        return pltpu.make_async_remote_copy(
            src_ref=part, dst_ref=part, send_sem=wide_send.at[j], recv_sem=wide_recv.at[j],
            device_id=place.partner, device_id_type=pl.DeviceIdType.MESH,
        )

    def subtract(turn, start):
        for t in range(TILES):
            rows = pl.ds(t * TILE, TILE)
            before = targets[rows, :].astype(F32) if start else left[rows, :]
            left[rows, :] = before - jnp.dot(feats[turn, rows, :], wh_out[turn], preferred_element_type=F32)

    arrived(0, 0)
    broadcast(0, product(0, 0, moment(0)))
    advance(N, N)
    assert all(done)
    arrived(0, 1)
    w1 = product(1, 0, moment(1))
    arrived(0, 2)
    w2 = product(2, 0, moment(2))
    for source in range(1, PLANES):
        arrived(1, source)
    all_but_one(0).wait_recv()
    broadcast(1, w1 - product2(1, 1, wh_out[0]))
    w2 = w2 - product2(2, 1, wh_out[0])
    subtract(0, True)
    all_but_one(1).wait_recv()
    broadcast(2, w2 - product2(3, 1, wh_out[1]))
    subtract(1, False)
    hand = pltpu.make_async_copy(left, left_out, store_sem.at[1])
    hand.start()
    all_but_one(2).wait_recv()
    for copy in copies:
        copy.wait_send()
    for k in range(2):
        @pl.when(sends[k])
        def _():
            for d in range(1, PLANES):
                slab_copy(k, plane, d).wait_send()

    for j in range(NBLK):
        all_but_one(j).wait_send()
    keep.wait()
    hand.wait()


def exchange_call(order, bounds, phases, data, projections, targets):
    vmem = pl.BlockSpec(memory_space=pltpu.VMEM)
    smem = pl.BlockSpec(memory_space=pltpu.SMEM)
    hbm = pl.BlockSpec(memory_space=pl.ANY)
    rows, classes = targets.shape
    buffers = []
    for _, height in CHUNKS:
        buffers += [
            pltpu.VMEM((height // 2, LANES), F32),
            pltpu.VMEM((height // 2, LANES), F32),
            pltpu.VMEM((2, 3, height // 16, LANES), F32),
            pltpu.VMEM((2, 3, height // 64, LANES), F32),
            pltpu.VMEM((height // 8, LANES), F32),
        ]
    dma = pltpu.SemaphoreType.DMA
    return pl.pallas_call(
        functools.partial(exchange_kernel, sine_coefficients(math.sqrt(2.0 / F))),
        in_specs=[smem, smem, vmem, hbm, hbm, hbm],
        out_specs=[vmem, vmem, hbm, hbm],
        out_shape=[
            jax.ShapeDtypeStruct((NBLK, SLAB, classes), F32),
            jax.ShapeDtypeStruct((NBLK, F, classes), BF),
            jax.ShapeDtypeStruct((rows, F), BF),
            jax.ShapeDtypeStruct((rows, classes), F32),
        ],
        scratch_shapes=[
            pltpu.VMEM(data.shape, BF),
            pltpu.VMEM(projections.shape, BF),
            pltpu.VMEM((data.shape[1], F), BF),
            pltpu.VMEM(targets.shape, BF),
            pltpu.VMEM((NBLK, rows, F), BF),
            pltpu.VMEM((rows, classes), F32),
            pltpu.VMEM((HEIGHT, LANES), F32),
            pltpu.VMEM((HEIGHT, LANES), F32),
            pltpu.VMEM((F, F), F32),
            pltpu.VMEM((PLANES, 2, SLAB, F), F32),
            *buffers,
            dma((len(CHUNKS), COPIES)),
            dma((len(CHUNKS), COPIES)),
            dma((2, PLANES)),
            dma((2, PLANES)),
            dma((NBLK,)),
            dma((NBLK,)),
            dma((2 + TILES,)),
            dma((2,)),
        ],
        compiler_params=pltpu.CompilerParams(collective_id=0, has_side_effects=True),
        name="exchange",
    )(order, bounds.T, phases, data, projections, targets)


def residual_kernel(order, w, feats_in, half_in, left_in, weights, residual, feats, half, left, result, load_sem, store_sem):
    tiles = left.shape[0] // RESIDUAL_TILE

    def rows(t):
        return pl.ds(t * RESIDUAL_TILE, RESIDUAL_TILE)

    loads = [pltpu.make_async_copy(half_in.at[NBLK - 1], half, load_sem.at[2 * tiles])]
    for t in range(tiles):
        loads.append(pltpu.make_async_copy(feats_in.at[rows(t)], feats.at[rows(t)], load_sem.at[2 * t]))
        loads.append(pltpu.make_async_copy(left_in.at[rows(t)], left.at[rows(t)], load_sem.at[2 * t + 1]))
    for copy in loads:
        copy.start()
    for turn in range(NBLK):
        weights[order[turn]] = w[turn]
    loads[0].wait()
    stores = []
    for t in range(tiles):
        loads[1 + 2 * t].wait()
        loads[2 + 2 * t].wait()
        product = jnp.dot(feats[rows(t), :], half[...], preferred_element_type=F32)
        result[rows(t), :] = left[rows(t), :] - product
        copy = pltpu.make_async_copy(result.at[rows(t)], residual.at[rows(t)], store_sem.at[t])
        copy.start()
        stores.append(copy)
    for copy in stores:
        copy.wait()


def residual_call(order, feats, half, left, w):
    rows, classes = left.shape
    vmem = pl.BlockSpec(memory_space=pltpu.VMEM)
    hbm = pl.BlockSpec(memory_space=pl.ANY)
    tiles = rows // RESIDUAL_TILE
    return pl.pallas_call(
        residual_kernel,
        in_specs=[pl.BlockSpec(memory_space=pltpu.SMEM), vmem, hbm, hbm, hbm],
        out_specs=[vmem, hbm],
        out_shape=[
            jax.ShapeDtypeStruct((NBLK, SLAB, classes), F32),
            jax.ShapeDtypeStruct((rows, classes), F32),
        ],
        scratch_shapes=[
            pltpu.VMEM((rows, F), BF),
            pltpu.VMEM((F, classes), BF),
            pltpu.VMEM((rows, classes), F32),
            pltpu.VMEM((rows, classes), F32),
            pltpu.SemaphoreType.DMA((2 * tiles + 1,)),
            pltpu.SemaphoreType.DMA((tiles,)),
        ],
        name="residual",
    )(order, w, feats, half, left)


def body(data, projections, phases, targets, bounds, order):
    w, half, feats, left = exchange_call(order, bounds, phases, data, projections, targets)
    weights, residual = residual_call(order, feats, half, left, w)
    return (weights, residual)


def solution(mesh):
    return jax.shard_map(
        body,
        mesh=mesh,
        in_specs=(P("rows", None), P(), P(), P("rows", "cls"), P(), P()),
        out_specs=(P(None, "rows", "cls"), P("rows", "cls")),
        check_vma=False,
    )
```

```python
import functools
import math

import jax
import jax.numpy as jnp
from jax import lax
from jax.experimental import pallas as pl
from jax.experimental.pallas import tpu as pltpu
from jax.sharding import PartitionSpec as P

F = 512
NBLK = 3
TILE = 512
RESIDUAL_TILE = 512
TILES = 4
SLAB = 16
BF = jnp.bfloat16
F32 = jnp.float32
LANES = 128
ROWS = 32
PLANES = 4
GRAM, CROSS, MOMENT, HEIGHT = 0, 3 * F, 7 * F, 13 * F
HALF = F // 2
TURN = 1.0 / (2.0 * math.pi)


def sine_coefficients(scale):
    import numpy as np

    nodes = np.cos((np.arange(64) + 0.5) * math.pi / 64)
    u = (nodes + 1) / 2 / 16
    a = np.sqrt(u)
    fit = np.polynomial.polynomial.polyfit(u, np.sin(2 * math.pi * a) / a, 3, w=a)
    return [float(c) * scale for c in fit]


def scaled_cosine(turns, coefficients):
    a = 0.25 - jnp.abs(turns - jnp.round(turns))
    u = a * a
    value = coefficients[-1]
    for c in coefficients[-2::-1]:
        value = value * u + c
    return value * a


def split(x):
    high = x.astype(BF)
    return high, (x - high.astype(F32)).astype(BF)


def dot3(left, right, dims=(((1,), (0,)), ((), ()))):
    lh, ll = left
    rh, rl = right
    dot = functools.partial(lax.dot_general, dimension_numbers=dims, preferred_element_type=F32)
    return dot(lh, rh) + (dot(lh, rl) + dot(ll, rh))


def mod4(v):
    return lax.rem(v + 8, 4)


class Place:
    def __init__(self):
        self.row = lax.axis_index("rows")
        self.plane = lax.axis_index("cls")
        self.core = lax.rem(self.row, 2)
        self.x = lax.rem(lax.div(self.row, 2), 4)
        self.y = lax.div(self.row, 8)
        self.partner = {"rows": self.row + 1 - 2 * self.core}

    def at(self, axis):
        return self.x if axis == "x" else self.y

    def near(self, axis, step):
        x = mod4(self.x + step) if axis == "x" else self.x
        y = mod4(self.y + step) if axis == "y" else self.y
        return {"rows": (y * 4 + x) * 2 + self.core}


def window(start, size):
    return pl.ds(pl.multiple_of(start, 8), size)


CHUNKS = (
    (GRAM, 3 * F, True),
    (CROSS, 4 * F, True),
    *((MOMENT + 2 * F * j, 2 * F, False) for j in range(NBLK)),
)
CHIP_SLAB = 2 * SLAB
CHIPS = ROWS // 2
COPIES = 27


def reduce_chunk(place, q, v, out, r0, acc, ring1, ring2, part1, send_sem, recv_sem, copies):
    base, height, join = CHUNKS[q]
    half = height // 2
    hops = [(part, d) for d in (2, 1, 3) for part in range(2)]

    def send(k, source, target, device):
        copy = pltpu.make_async_remote_copy(
            src_ref=source, dst_ref=target, send_sem=send_sem.at[q, k], recv_sem=recv_sem.at[q, k],
            device_id=device, device_id_type=pl.DeviceIdType.MESH,
        )
        copy.start()
        copies.append(copy)
        return copy

    first = send(0, v.at[window(base + (1 - place.core) * half, half)], r0, place.partner)
    yield
    first.wait_recv()
    acc[...] = v[window(base + place.core * half, half), :] + r0[...]

    def scatter(k, axes, source, origin, size, ring, store):
        flights = {}
        for part, d in hops:
            target = mod4(place.at(axes[part]) + d)
            piece = source.at[window(origin(part) + target * size, size)]
            flights[part, d] = send(k + part * 3 + d - 1, piece, ring.at[part, d - 1], place.near(axes[part], d))
        yield
        for part in range(2):
            total = source[window(origin(part) + place.at(axes[part]) * size, size), :]
            for d in range(1, 4):
                flights[part, d].wait_recv()
                total = total + ring[part, d - 1]
            store(part, total)

    def gather(k, axes, origin, size):
        flights = []
        for part, d in hops:
            mine = out.at[window(base + origin(part) + place.at(axes[part]) * size, size)]
            flights.append(send(k + part * 3 + d - 1, mine, mine, place.near(axes[part], d)))
        yield
        for copy in flights:
            copy.wait_recv()

    one, two = ("x", "y"), ("y", "x")
    quarter, sixteenth, last = height // 4, height // 16, height // 64

    def store1(part, value):
        part1[part * sixteenth:(part + 1) * sixteenth, :] = value

    yield from scatter(1, one, acc, lambda part: part * quarter, sixteenth, ring1, store1)

    def own(part):
        return place.core * half + part * quarter + place.at(one[part]) * sixteenth

    def store2(part, value):
        out[window(base + own(part) + place.at(two[part]) * last, last), :] = value

    yield from scatter(7, two, part1, lambda part: part * sixteenth, last, ring2, store2)
    yield from gather(13, two, own, last)
    yield from gather(19, one, lambda part: place.core * half + part * quarter, sixteenth)
    if not join:
        return
    finals = []
    for part in range(2):
        mine = out.at[window(base + place.core * half + part * quarter, quarter)]
        finals.append(send(25 + part, mine, mine, place.partner))
    yield
    for copy in finals:
        copy.wait_recv()


def exchange_kernel(
    coefficients, order, bounds, phases, data_in, proj_in, targets_in, w_out, wh_out, feats_out, left_out,
    data, proj, chosen, targets, feats, left, v, out, s1, slabs, wh, parts, other, *scratch
):
    place = Place()
    buffers = scratch[:5 * len(CHUNKS)]
    send_sem, recv_sem, plane_send, plane_recv, wide_send, wide_recv, pair_send, pair_recv, load_sem, store_sem = (
        scratch[5 * len(CHUNKS):]
    )
    me, plane = place.row, place.plane
    height = data.shape[0]
    loads = [pltpu.make_async_copy(proj_in, proj, load_sem.at[0])]
    for t in range(TILES):
        rows = pl.ds(t * TILE, TILE)
        loads.append(pltpu.make_async_copy(data_in.at[rows], data.at[rows], load_sem.at[1 + t]))
    loads.append(pltpu.make_async_copy(targets_in, targets, load_sem.at[1 + TILES]))
    for copy in loads:
        copy.start()

    barrier = pltpu.get_barrier_semaphore()

    greeted = [place.partner]
    greeted += [place.near(axis, d) for axis in ("x", "y") for d in range(1, 4)]
    greeted += [{"cls": lax.rem(plane + d, PLANES)} for d in range(1, PLANES)]
    for device in greeted:
        pl.semaphore_signal(barrier, inc=1, device_id=device, device_id_type=pl.DeviceIdType.MESH)

    copies = []
    runs = [
        reduce_chunk(place, q, v, out, *buffers[5 * q:5 * q + 5], send_sem, recv_sem, copies)
        for q in range(len(CHUNKS))
    ]
    done = [False] * len(runs)

    def advance(*which):
        for q in which:
            if not done[q]:
                try:
                    next(runs[q])
                except StopIteration:
                    done[q] = True

    turn_a = jnp.minimum(plane, 2)
    turn_b = jnp.where(plane == 0, 1, 0)
    turn_c = 3 - turn_a - turn_b
    turn_x = jnp.where(plane == 3, 1, 0)
    contract = (((0,), (0,)), ((), ()))

    def pick(turn, values):
        block = order[turn]
        return jnp.where(block == 0, values[0], jnp.where(block == 1, values[1], values[2]))

    def columns(ref):
        return [ref[:, j * F:(j + 1) * F] for j in range(NBLK)]

    def choose(turn):
        chosen[...] = pick(turn, columns(proj))

    def features(turn, tiles):
        shift = pick(turn, [phases[j * F:(j + 1) * F] for j in range(NBLK)])[None, :] * TURN
        for t in tiles:
            rows = pl.ds(t * TILE, TILE)
            angle = jnp.dot(data[rows, :], chosen[...], preferred_element_type=F32)
            feats[turn, rows, :] = scaled_cosine(angle * TURN + shift, coefficients).astype(BF)

    def put(base, value):
        tall, width = value.shape
        for k in range(width // LANES):
            v[window(base + k * tall, tall), :] = value[:, k * LANES:(k + 1) * LANES]

    def moments(turn):
        put(MOMENT + 2 * F * turn, lax.dot_general(feats[turn], targets[...], contract, preferred_element_type=F32))

    def gram():
        for n in range(2):
            lhs = feats[turn_a, :, n * HALF:(n + 1) * HALF]
            rhs = feats[turn_a, :, n * HALF:]
            put(GRAM + n * 2 * F, lax.dot_general(lhs, rhs, contract, preferred_element_type=F32))

    G, C, M0, M1, M2 = range(5)
    loads[0].wait()
    choose(turn_a)
    for t in range(TILES):
        loads[1 + t].wait()
        features(turn_a, [t])
    gram()
    pl.semaphore_wait(barrier, len(greeted))
    choose(turn_b)
    features(turn_b, [0])
    advance(G)
    features(turn_b, [1])
    features(turn_b, [2])
    features(turn_b, [3])
    advance(G)
    loads[1 + TILES].wait()
    moments(0)
    choose(turn_c)
    features(turn_c, [0])
    advance(M0)
    features(turn_c, [1])
    features(turn_c, [2])
    features(turn_c, [3])
    put(CROSS, lax.dot_general(feats[turn_a], feats[turn_x], contract, preferred_element_type=F32))
    advance(C, M0)
    moments(1)
    advance(M1, G, C, M0, G, M1, C, M0, G)
    moments(2)
    keep = pltpu.make_async_copy(feats.at[NBLK - 1], feats_out, store_sem.at[0])
    keep.start()
    advance(M2, M1, C, M2, M0, G, M1, C, G)

    def wide(base, width, tall=F):
        return jnp.concatenate([out[window(base + k * tall, tall), :] for k in range(width // LANES)], axis=1)

    lower = jnp.full((1, F), pick(turn_a, [bounds[0, j] for j in range(NBLK)]), F32)
    upper = jnp.full((1, F), pick(turn_a, [bounds[1, j] for j in range(NBLK)]), F32)
    center = 0.5 * (upper + lower)
    u = 0.5 * (upper - lower) / center
    k1 = 2.0 / (2.0 - u * u)
    u = u * u / (2.0 - u * u)
    k2 = 2.0 / (2.0 - u * u)
    u = u * u / (2.0 - u * u)
    k4 = 2.0 / (2.0 - u * u)
    u = u * u / (2.0 - u * u)
    k8 = 2.0 / (2.0 - u * u)
    scale = 1.0 / (center * (height * ROWS))

    eye = (
        lax.broadcasted_iota(jnp.int32, (F, F), 0) == lax.broadcasted_iota(jnp.int32, (F, F), 1)
    ).astype(F32)
    top = wide(GRAM, F, HALF)
    corner = wide(GRAM + 2 * F, HALF, HALF)
    whole = jnp.concatenate([top, jnp.concatenate([top[:, HALF:].T, corner], axis=1)], axis=0)
    first = whole * scale + eye * (lower / center)
    s1[...] = first
    chip = lax.div(me, 2)
    row = lax.broadcasted_iota(jnp.int32, (CHIP_SLAB, F), 0) + chip * CHIP_SLAB
    column = lax.broadcasted_iota(jnp.int32, (CHIP_SLAB, F), 1)
    unit = (row == column).astype(F32)
    value = k1 * (2.0 * unit - s1[window(chip * CHIP_SLAB, CHIP_SLAB), :])
    part1 = split(first)
    second = k1 * (2.0 * first - dot3(part1, part1))
    part2 = split(second)
    value = k2 * (2.0 * value - dot3(split(value), part2))
    fourth = k2 * (2.0 * second - dot3(part2, part2))
    part4 = split(fourth)
    value = k4 * (2.0 * value - dot3(split(value), part4))
    once = dot3(split(value), part4)
    value = k8 * (2.0 * value - k4 * (2.0 * once - dot3(split(once), part4)))
    value = value * scale

    inner = jnp.logical_and(plane != 0, plane != PLANES - 1)
    edge = plane == 0

    def slab_copy(k, source, d):
        return pltpu.make_async_remote_copy(
            src_ref=slabs.at[source, k], dst_ref=slabs.at[source, k],
            send_sem=plane_send.at[k, d], recv_sem=plane_recv.at[k, source],
            device_id={"cls": lax.rem(plane + d, PLANES)}, device_id_type=pl.DeviceIdType.MESH,
        )

    def cross_planes(k, sends):
        @pl.when(sends)
        def _():
            for d in (2, 1, 3):
                slab_copy(k, plane, d).start()

    def arrived(k, source):
        @pl.when(plane != source)
        def _():
            slab_copy(k, source, 1).wait_recv()

    slabs[plane, 0] = value
    cross_planes(0, edge)
    advance(M2, M0, M1, C, M2, C)
    slabs[plane, 1] = dot3(split(value), split(wide(CROSS, F)))
    cross_planes(1, plane != 0)
    cross_planes(0, inner)

    def moment(j):
        return split(out[window(MOMENT + 2 * F * j + place.core * F, F), :])

    def product(z, k, right):
        return dot3(split(slabs[z, k]), right)

    def product2(z, k, right):
        high, low = split(slabs[z, k])
        return jnp.dot(high, right, preferred_element_type=F32) + jnp.dot(low, right, preferred_element_type=F32)

    def half(j):
        return wh[j, place.core]

    def pair_copy(n, ref):
        return pltpu.make_async_remote_copy(
            src_ref=ref, dst_ref=ref, send_sem=pair_send.at[n], recv_sem=pair_recv.at[n],
            device_id=place.partner, device_id_type=pl.DeviceIdType.MESH,
        )

    far_first = sorted(
        ((dx, dy) for dx in range(4) for dy in range(4)),
        key=lambda hop: -(min(hop[0], 4 - hop[0]) + min(hop[1], 4 - hop[1])),
    )

    def broadcast(j, w):
        parts[place.core, j] = w[:SLAB]
        other[j] = w[SLAB:]

        @pl.when(place.core == 1)
        def _():
            parts[place.core, j] = w[SLAB:]
            other[j] = w[:SLAB]

        mine = wh.at[j, place.core, pl.ds(pl.multiple_of(chip * CHIP_SLAB, CHIP_SLAB), CHIP_SLAB)]
        wh[j, place.core, pl.ds(pl.multiple_of(chip * CHIP_SLAB, CHIP_SLAB), CHIP_SLAB), :] = w.astype(BF)
        for dx, dy in far_first:
            there = (mod4(place.y + dy) * 4 + mod4(place.x + dx)) * 2
            for swap in range(2 if j == NBLK - 1 else 1):
                if dx == 0 and dy == 0 and swap == 0:
                    continue
                core = 1 - place.core if swap else place.core
                pltpu.make_async_remote_copy(
                    src_ref=mine, dst_ref=mine, send_sem=wide_send.at[j + swap], recv_sem=wide_recv.at[j + swap],
                    device_id={"rows": there + core}, device_id_type=pl.DeviceIdType.MESH,
                ).start()

    def received(n):
        j = min(n, NBLK - 1)
        part = wh.at[j, 0, pl.ds(0, F if n == NBLK else F - CHIP_SLAB)]
        return pltpu.make_async_remote_copy(
            src_ref=part, dst_ref=part, send_sem=wide_send.at[n], recv_sem=wide_recv.at[n],
            device_id=place.partner, device_id_type=pl.DeviceIdType.MESH,
        )

    def whole_half(j):
        return jnp.concatenate([wh[j, 0], wh[j, 1]], axis=1)

    def subtract(turn, start):
        both = whole_half(turn)
        for t in range(TILES):
            rows = pl.ds(t * TILE, TILE)
            before = targets[rows, :].astype(F32) if start else left[rows, :]
            left[rows, :] = before - jnp.dot(feats[turn, rows, :], both, preferred_element_type=F32)

    arrived(0, 0)
    broadcast(0, product(0, 0, moment(0)))
    advance(M1, M2)
    arrived(0, 1)
    w1 = product(1, 0, moment(1))
    for source in range(1, PLANES):
        arrived(1, source)
    received(0).wait_recv()
    w1 = w1 - product2(1, 1, half(0))
    broadcast(1, w1)
    advance(M2)
    assert all(done)
    swaps = [pair_copy(0, wh.at[0, place.core])]
    swaps[0].start()
    arrived(0, 2)
    w2 = product(2, 0, moment(2)) - product2(2, 1, half(0))
    swaps[0].wait_recv()
    subtract(0, True)
    received(1).wait_recv()
    broadcast(2, w2 - product2(3, 1, half(1)))
    swaps.append(pair_copy(1, wh.at[1, place.core]))
    swaps[1].start()
    give = pltpu.make_async_remote_copy(
        src_ref=other, dst_ref=parts.at[place.core], send_sem=pair_send.at[2], recv_sem=pair_recv.at[2],
        device_id=place.partner, device_id_type=pl.DeviceIdType.MESH,
    )
    give.start()
    swaps[1].wait_recv()
    subtract(1, False)
    hand = pltpu.make_async_copy(left, left_out, store_sem.at[1])
    hand.start()
    give.wait_recv()
    w_out[...] = parts[...]
    received(2).wait_recv()
    received(NBLK).wait_recv()
    wh_out[...] = whole_half(NBLK - 1)
    for copy in copies + swaps + [give]:
        copy.wait_send()
    for k, sends in ((0, plane != PLANES - 1), (1, plane != 0)):
        @pl.when(sends)
        def _():
            for d in range(1, PLANES):
                slab_copy(k, plane, d).wait_send()

    for n in range(NBLK + 1):
        received(n).wait_send()
    keep.wait()
    hand.wait()


def exchange_call(order, bounds, phases, data, projections, targets):
    vmem = pl.BlockSpec(memory_space=pltpu.VMEM)
    smem = pl.BlockSpec(memory_space=pltpu.SMEM)
    hbm = pl.BlockSpec(memory_space=pl.ANY)
    rows, classes = targets.shape
    buffers = []
    for _, height, _ in CHUNKS:
        buffers += [
            pltpu.VMEM((height // 2, LANES), F32),
            pltpu.VMEM((height // 2, LANES), F32),
            pltpu.VMEM((2, 3, height // 16, LANES), F32),
            pltpu.VMEM((2, 3, height // 64, LANES), F32),
            pltpu.VMEM((height // 8, LANES), F32),
        ]
    dma = pltpu.SemaphoreType.DMA
    return pl.pallas_call(
        functools.partial(exchange_kernel, sine_coefficients(math.sqrt(2.0 / F))),
        in_specs=[smem, smem, vmem, hbm, hbm, hbm],
        out_specs=[vmem, vmem, hbm, hbm],
        out_shape=[
            jax.ShapeDtypeStruct((2, NBLK, SLAB, LANES), F32),
            jax.ShapeDtypeStruct((F, classes), BF),
            jax.ShapeDtypeStruct((rows, F), BF),
            jax.ShapeDtypeStruct((rows, classes), F32),
        ],
        scratch_shapes=[
            pltpu.VMEM(data.shape, BF),
            pltpu.VMEM(projections.shape, BF),
            pltpu.VMEM((data.shape[1], F), BF),
            pltpu.VMEM(targets.shape, BF),
            pltpu.VMEM((NBLK, rows, F), BF),
            pltpu.VMEM((rows, classes), F32),
            pltpu.VMEM((HEIGHT, LANES), F32),
            pltpu.VMEM((HEIGHT, LANES), F32),
            pltpu.VMEM((F, F), F32),
            pltpu.VMEM((PLANES, 2, CHIP_SLAB, F), F32),
            pltpu.VMEM((NBLK, 2, F, LANES), BF),
            pltpu.VMEM((2, NBLK, SLAB, LANES), F32),
            pltpu.VMEM((NBLK, SLAB, LANES), F32),
            *buffers,
            dma((len(CHUNKS), COPIES)),
            dma((len(CHUNKS), COPIES)),
            dma((2, PLANES)),
            dma((2, PLANES)),
            dma((NBLK + 1,)),
            dma((NBLK + 1,)),
            dma((NBLK,)),
            dma((NBLK,)),
            dma((2 + TILES,)),
            dma((2,)),
        ],
        compiler_params=pltpu.CompilerParams(collective_id=0, has_side_effects=True),
        name="exchange",
    )(order, bounds.T, phases, data, projections, targets)


def residual_kernel(order, w, feats_in, half_in, left_in, weights, residual, feats, half, left, result, load_sem, store_sem):
    tiles = left.shape[0] // RESIDUAL_TILE

    def rows(t):
        return pl.ds(t * RESIDUAL_TILE, RESIDUAL_TILE)

    loads = [pltpu.make_async_copy(half_in, half, load_sem.at[2 * tiles])]
    for t in range(tiles):
        loads.append(pltpu.make_async_copy(feats_in.at[rows(t)], feats.at[rows(t)], load_sem.at[2 * t]))
        loads.append(pltpu.make_async_copy(left_in.at[rows(t)], left.at[rows(t)], load_sem.at[2 * t + 1]))
    for copy in loads:
        copy.start()
    for turn in range(NBLK):
        weights[order[turn]] = jnp.concatenate([w[0, turn], w[1, turn]], axis=1)
    loads[0].wait()
    stores = []
    for t in range(tiles):
        loads[1 + 2 * t].wait()
        loads[2 + 2 * t].wait()
        product = jnp.dot(feats[rows(t), :], half[...], preferred_element_type=F32)
        result[rows(t), :] = left[rows(t), :] - product
        copy = pltpu.make_async_copy(result.at[rows(t)], residual.at[rows(t)], store_sem.at[t])
        copy.start()
        stores.append(copy)
    for copy in stores:
        copy.wait()


def residual_call(order, feats, half, left, w):
    rows, classes = left.shape
    vmem = pl.BlockSpec(memory_space=pltpu.VMEM)
    hbm = pl.BlockSpec(memory_space=pl.ANY)
    tiles = rows // RESIDUAL_TILE
    return pl.pallas_call(
        residual_kernel,
        in_specs=[pl.BlockSpec(memory_space=pltpu.SMEM), vmem, hbm, hbm, hbm],
        out_specs=[vmem, hbm],
        out_shape=[
            jax.ShapeDtypeStruct((NBLK, SLAB, classes), F32),
            jax.ShapeDtypeStruct((rows, classes), F32),
        ],
        scratch_shapes=[
            pltpu.VMEM((rows, F), BF),
            pltpu.VMEM((F, classes), BF),
            pltpu.VMEM((rows, classes), F32),
            pltpu.VMEM((rows, classes), F32),
            pltpu.SemaphoreType.DMA((2 * tiles + 1,)),
            pltpu.SemaphoreType.DMA((tiles,)),
        ],
        name="residual",
    )(order, w, feats, half, left)


def body(data, projections, phases, targets, bounds, order):
    w, half, feats, left = exchange_call(order, bounds, phases, data, projections, targets)
    weights, residual = residual_call(order, feats, half, left, w)
    return (weights, residual)


def solution(mesh):
    return jax.shard_map(
        body,
        mesh=mesh,
        in_specs=(P("rows", None), P(), P(), P("rows", "cls"), P(), P()),
        out_specs=(P(None, "rows", "cls"), P("rows", "cls")),
        check_vma=False,
    )
```

```python
import functools
import math

import jax
import jax.numpy as jnp
from jax import lax
from jax.experimental import pallas as pl
from jax.experimental.pallas import tpu as pltpu
from jax.sharding import PartitionSpec as P

F = 512
NBLK = 3
TILE = 512
RESIDUAL_TILE = 512
TILES = 4
SLAB = 16
BF = jnp.bfloat16
F32 = jnp.float32
LANES = 128
ROWS = 32
PLANES = 4
GRAM, CROSS, MOMENT, HEIGHT = 0, 3 * F, 7 * F, 13 * F
HALF = F // 2
TURN = 1.0 / (2.0 * math.pi)


def sine_coefficients(scale):
    import numpy as np

    nodes = np.cos((np.arange(64) + 0.5) * math.pi / 64)
    u = (nodes + 1) / 2 / 16
    a = np.sqrt(u)
    fit = np.polynomial.polynomial.polyfit(u, np.sin(2 * math.pi * a) / a, 3, w=a)
    return [float(c) * scale for c in fit]


def scaled_cosine(turns, coefficients):
    a = 0.25 - jnp.abs(turns - jnp.round(turns))
    u = a * a
    value = coefficients[-1]
    for c in coefficients[-2::-1]:
        value = value * u + c
    return value * a


def split(x):
    high = x.astype(BF)
    return high, (x - high.astype(F32)).astype(BF)


def dot3(left, right, dims=(((1,), (0,)), ((), ()))):
    lh, ll = left
    rh, rl = right
    dot = functools.partial(lax.dot_general, dimension_numbers=dims, preferred_element_type=F32)
    return dot(lh, rh) + (dot(lh, rl) + dot(ll, rh))


def mod4(v):
    return lax.rem(v + 8, 4)


class Place:
    def __init__(self):
        self.row = lax.axis_index("rows")
        self.plane = lax.axis_index("cls")
        self.core = lax.rem(self.row, 2)
        self.x = lax.rem(lax.div(self.row, 2), 4)
        self.y = lax.div(self.row, 8)
        self.partner = {"rows": self.row + 1 - 2 * self.core}

    def at(self, axis):
        return self.x if axis == "x" else self.y

    def near(self, axis, step):
        x = mod4(self.x + step) if axis == "x" else self.x
        y = mod4(self.y + step) if axis == "y" else self.y
        return {"rows": (y * 4 + x) * 2 + self.core}


def window(start, size):
    return pl.ds(pl.multiple_of(start, 8), size)


CHUNKS = (
    (GRAM, 3 * F, True),
    (CROSS, 4 * F, True),
    *((MOMENT + 2 * F * j, 2 * F, False) for j in range(NBLK)),
)
CHIP_SLAB = 2 * SLAB
CHIPS = ROWS // 2
COPIES = 27


def reduce_chunk(place, q, v, out, r0, acc, ring1, ring2, part1, send_sem, recv_sem, copies):
    base, height, join = CHUNKS[q]
    half = height // 2
    hops = [(part, d) for d in (2, 1, 3) for part in range(2)]

    def send(k, source, target, device):
        copy = pltpu.make_async_remote_copy(
            src_ref=source, dst_ref=target, send_sem=send_sem.at[q, k], recv_sem=recv_sem.at[q, k],
            device_id=device, device_id_type=pl.DeviceIdType.MESH,
        )
        copy.start()
        copies.append(copy)
        return copy

    first = send(0, v.at[window(base + (1 - place.core) * half, half)], r0, place.partner)
    yield
    first.wait_recv()
    acc[...] = v[window(base + place.core * half, half), :] + r0[...]

    def scatter(k, axes, source, origin, size, ring, store):
        flights = {}
        for part, d in hops:
            target = mod4(place.at(axes[part]) + d)
            piece = source.at[window(origin(part) + target * size, size)]
            flights[part, d] = send(k + part * 3 + d - 1, piece, ring.at[part, d - 1], place.near(axes[part], d))
        yield
        for part in range(2):
            total = source[window(origin(part) + place.at(axes[part]) * size, size), :]
            for d in range(1, 4):
                flights[part, d].wait_recv()
                total = total + ring[part, d - 1]
            store(part, total)

    def gather(k, axes, origin, size):
        flights = []
        for part, d in hops:
            mine = out.at[window(base + origin(part) + place.at(axes[part]) * size, size)]
            flights.append(send(k + part * 3 + d - 1, mine, mine, place.near(axes[part], d)))
        yield
        for copy in flights:
            copy.wait_recv()

    one, two = ("x", "y"), ("y", "x")
    quarter, sixteenth, last = height // 4, height // 16, height // 64

    def store1(part, value):
        part1[part * sixteenth:(part + 1) * sixteenth, :] = value

    yield from scatter(1, one, acc, lambda part: part * quarter, sixteenth, ring1, store1)

    def own(part):
        return place.core * half + part * quarter + place.at(one[part]) * sixteenth

    def store2(part, value):
        out[window(base + own(part) + place.at(two[part]) * last, last), :] = value

    yield from scatter(7, two, part1, lambda part: part * sixteenth, last, ring2, store2)
    yield from gather(13, two, own, last)
    yield from gather(19, one, lambda part: place.core * half + part * quarter, sixteenth)
    if not join:
        return
    finals = []
    for part in range(2):
        mine = out.at[window(base + place.core * half + part * quarter, quarter)]
        finals.append(send(25 + part, mine, mine, place.partner))
    yield
    for copy in finals:
        copy.wait_recv()


def exchange_kernel(
    coefficients, order, bounds, phases, data_in, proj_in, targets_in, w_out, wh_out, feats_out, left_out,
    data, proj, chosen, targets, feats, left, v, out, s1, slabs, wh, parts, other, *scratch
):
    place = Place()
    buffers = scratch[:5 * len(CHUNKS)]
    send_sem, recv_sem, plane_send, plane_recv, wide_send, wide_recv, pair_send, pair_recv, load_sem, store_sem = (
        scratch[5 * len(CHUNKS):]
    )
    me, plane = place.row, place.plane
    height = data.shape[0]
    loads = [pltpu.make_async_copy(proj_in, proj, load_sem.at[0])]
    for t in range(TILES):
        rows = pl.ds(t * TILE, TILE)
        loads.append(pltpu.make_async_copy(data_in.at[rows], data.at[rows], load_sem.at[1 + t]))
    loads.append(pltpu.make_async_copy(targets_in, targets, load_sem.at[1 + TILES]))
    for copy in loads[:3]:
        copy.start()

    barrier = pltpu.get_barrier_semaphore()

    greeted = [place.partner]
    greeted += [place.near(axis, d) for axis in ("x", "y") for d in range(1, 4)]
    greeted += [{"cls": lax.rem(plane + d, PLANES)} for d in range(1, PLANES)]
    for device in greeted:
        pl.semaphore_signal(barrier, inc=1, device_id=device, device_id_type=pl.DeviceIdType.MESH)

    copies = []
    runs = [
        reduce_chunk(place, q, v, out, *buffers[5 * q:5 * q + 5], send_sem, recv_sem, copies)
        for q in range(len(CHUNKS))
    ]
    done = [False] * len(runs)

    def advance(*which):
        for q in which:
            if not done[q]:
                try:
                    next(runs[q])
                except StopIteration:
                    done[q] = True

    turn_a = jnp.minimum(plane, 2)
    turn_b = jnp.where(plane == 0, 1, 0)
    turn_c = 3 - turn_a - turn_b
    turn_x = jnp.where(plane == 3, 1, 0)
    contract = (((0,), (0,)), ((), ()))

    def pick(turn, values):
        block = order[turn]
        return jnp.where(block == 0, values[0], jnp.where(block == 1, values[1], values[2]))

    def columns(ref):
        return [ref[:, j * F:(j + 1) * F] for j in range(NBLK)]

    def choose(turn):
        chosen[...] = pick(turn, columns(proj))

    def features(turn, tiles):
        shift = pick(turn, [phases[j * F:(j + 1) * F] for j in range(NBLK)])[None, :] * TURN
        for t in tiles:
            rows = pl.ds(t * TILE, TILE)
            angle = jnp.dot(data[rows, :], chosen[...], preferred_element_type=F32)
            feats[turn, rows, :] = scaled_cosine(angle * TURN + shift, coefficients).astype(BF)

    def put(base, value):
        tall, width = value.shape
        for k in range(width // LANES):
            v[window(base + k * tall, tall), :] = value[:, k * LANES:(k + 1) * LANES]

    def moments(turn):
        put(MOMENT + 2 * F * turn, lax.dot_general(feats[turn], targets[...], contract, preferred_element_type=F32))

    def gram():
        for n in range(2):
            lhs = feats[turn_a, :, n * HALF:(n + 1) * HALF]
            rhs = feats[turn_a, :, n * HALF:]
            put(GRAM + n * 2 * F, lax.dot_general(lhs, rhs, contract, preferred_element_type=F32))

    G, C, M0, M1, M2 = range(5)
    loads[0].wait()
    for copy in loads[3:]:
        copy.start()
    choose(turn_a)
    for t in range(TILES):
        loads[1 + t].wait()
        features(turn_a, [t])
    gram()
    pl.semaphore_wait(barrier, len(greeted))
    choose(turn_b)
    features(turn_b, [0])
    advance(G)
    features(turn_b, [1])
    features(turn_b, [2])
    features(turn_b, [3])
    advance(G)
    loads[1 + TILES].wait()
    moments(0)
    choose(turn_c)
    features(turn_c, [0])
    advance(M0)
    features(turn_c, [1])
    features(turn_c, [2])
    features(turn_c, [3])
    put(CROSS, lax.dot_general(feats[turn_a], feats[turn_x], contract, preferred_element_type=F32))
    advance(C, M0)
    moments(1)
    advance(M1, G, C, M0, G, M1, C, M0, G)
    moments(2)
    keep = pltpu.make_async_copy(feats.at[NBLK - 1], feats_out, store_sem.at[0])
    keep.start()
    advance(M2, M1, C, M2, M0, G, M1, C, G)

    def wide(base, width, tall=F):
        return jnp.concatenate([out[window(base + k * tall, tall), :] for k in range(width // LANES)], axis=1)

    lower = jnp.full((1, F), pick(turn_a, [bounds[0, j] for j in range(NBLK)]), F32)
    upper = jnp.full((1, F), pick(turn_a, [bounds[1, j] for j in range(NBLK)]), F32)
    center = 0.5 * (upper + lower)
    u = 0.5 * (upper - lower) / center
    k1 = 2.0 / (2.0 - u * u)
    u = u * u / (2.0 - u * u)
    k2 = 2.0 / (2.0 - u * u)
    u = u * u / (2.0 - u * u)
    k4 = 2.0 / (2.0 - u * u)
    u = u * u / (2.0 - u * u)
    k8 = 2.0 / (2.0 - u * u)
    scale = 1.0 / (center * (height * ROWS))

    eye = (
        lax.broadcasted_iota(jnp.int32, (F, F), 0) == lax.broadcasted_iota(jnp.int32, (F, F), 1)
    ).astype(F32)
    top = wide(GRAM, F, HALF)
    corner = wide(GRAM + 2 * F, HALF, HALF)
    whole = jnp.concatenate([top, jnp.concatenate([top[:, HALF:].T, corner], axis=1)], axis=0)
    first = whole * scale + eye * (lower / center)
    s1[...] = first
    chip = lax.div(me, 2)
    row = lax.broadcasted_iota(jnp.int32, (CHIP_SLAB, F), 0) + chip * CHIP_SLAB
    column = lax.broadcasted_iota(jnp.int32, (CHIP_SLAB, F), 1)
    unit = (row == column).astype(F32)
    value = k1 * (2.0 * unit - s1[window(chip * CHIP_SLAB, CHIP_SLAB), :])
    part1 = split(first)
    second = k1 * (2.0 * first - dot3(part1, part1))
    part2 = split(second)
    value = k2 * (2.0 * value - dot3(split(value), part2))
    fourth = k2 * (2.0 * second - dot3(part2, part2))
    part4 = split(fourth)
    value = k4 * (2.0 * value - dot3(split(value), part4))
    once = dot3(split(value), part4)
    value = k8 * (2.0 * value - k4 * (2.0 * once - dot3(split(once), part4)))
    value = value * scale

    inner = jnp.logical_and(plane != 0, plane != PLANES - 1)
    edge = plane == 0

    def slab_copy(k, source, d):
        return pltpu.make_async_remote_copy(
            src_ref=slabs.at[source, k], dst_ref=slabs.at[source, k],
            send_sem=plane_send.at[k, d], recv_sem=plane_recv.at[k, source],
            device_id={"cls": lax.rem(plane + d, PLANES)}, device_id_type=pl.DeviceIdType.MESH,
        )

    def cross_planes(k, sends):
        @pl.when(sends)
        def _():
            for d in (2, 1, 3):
                slab_copy(k, plane, d).start()

    def arrived(k, source):
        @pl.when(plane != source)
        def _():
            slab_copy(k, source, 1).wait_recv()

    slabs[plane, 0] = value
    cross_planes(0, edge)
    advance(M2, M0, M1, C, M2, C)
    slabs[plane, 1] = dot3(split(value), split(wide(CROSS, F)))
    cross_planes(1, plane != 0)
    cross_planes(0, inner)

    def moment(j):
        return split(out[window(MOMENT + 2 * F * j + place.core * F, F), :])

    def product(z, k, right):
        return dot3(split(slabs[z, k]), right)

    def product2(z, k, right):
        high, low = split(slabs[z, k])
        return jnp.dot(high, right, preferred_element_type=F32) + jnp.dot(low, right, preferred_element_type=F32)

    def half(j):
        return wh[j, place.core]

    def pair_copy(n, ref):
        return pltpu.make_async_remote_copy(
            src_ref=ref, dst_ref=ref, send_sem=pair_send.at[n], recv_sem=pair_recv.at[n],
            device_id=place.partner, device_id_type=pl.DeviceIdType.MESH,
        )

    far_first = sorted(
        ((dx, dy) for dx in range(4) for dy in range(4)),
        key=lambda hop: -(min(hop[0], 4 - hop[0]) + min(hop[1], 4 - hop[1])),
    )

    def broadcast(j, w):
        parts[place.core, j] = w[:SLAB]
        other[j] = w[SLAB:]

        @pl.when(place.core == 1)
        def _():
            parts[place.core, j] = w[SLAB:]
            other[j] = w[:SLAB]

        mine = wh.at[j, place.core, pl.ds(pl.multiple_of(chip * CHIP_SLAB, CHIP_SLAB), CHIP_SLAB)]
        wh[j, place.core, pl.ds(pl.multiple_of(chip * CHIP_SLAB, CHIP_SLAB), CHIP_SLAB), :] = w.astype(BF)
        for dx, dy in far_first:
            there = (mod4(place.y + dy) * 4 + mod4(place.x + dx)) * 2
            for swap in range(2 if j == NBLK - 1 else 1):
                if dx == 0 and dy == 0 and swap == 0:
                    continue
                core = 1 - place.core if swap else place.core
                pltpu.make_async_remote_copy(
                    src_ref=mine, dst_ref=mine, send_sem=wide_send.at[j + swap], recv_sem=wide_recv.at[j + swap],
                    device_id={"rows": there + core}, device_id_type=pl.DeviceIdType.MESH,
                ).start()

    def received(n):
        j = min(n, NBLK - 1)
        part = wh.at[j, 0, pl.ds(0, F if n == NBLK else F - CHIP_SLAB)]
        return pltpu.make_async_remote_copy(
            src_ref=part, dst_ref=part, send_sem=wide_send.at[n], recv_sem=wide_recv.at[n],
            device_id=place.partner, device_id_type=pl.DeviceIdType.MESH,
        )

    def whole_half(j):
        return jnp.concatenate([wh[j, 0], wh[j, 1]], axis=1)

    def subtract(turn, start):
        both = whole_half(turn)
        for t in range(TILES):
            rows = pl.ds(t * TILE, TILE)
            before = targets[rows, :].astype(F32) if start else left[rows, :]
            left[rows, :] = before - jnp.dot(feats[turn, rows, :], both, preferred_element_type=F32)

    arrived(0, 0)
    broadcast(0, product(0, 0, moment(0)))
    advance(M1, M2)
    arrived(0, 1)
    w1 = product(1, 0, moment(1))
    for source in range(1, PLANES):
        arrived(1, source)
    received(0).wait_recv()
    w1 = w1 - product2(1, 1, half(0))
    broadcast(1, w1)
    advance(M2)
    assert all(done)
    swaps = [pair_copy(0, wh.at[0, place.core])]
    swaps[0].start()
    arrived(0, 2)
    w2 = product(2, 0, moment(2)) - product2(2, 1, half(0))
    swaps[0].wait_recv()
    subtract(0, True)
    received(1).wait_recv()
    broadcast(2, w2 - product2(3, 1, half(1)))
    swaps.append(pair_copy(1, wh.at[1, place.core]))
    swaps[1].start()
    give = pltpu.make_async_remote_copy(
        src_ref=other, dst_ref=parts.at[place.core], send_sem=pair_send.at[2], recv_sem=pair_recv.at[2],
        device_id=place.partner, device_id_type=pl.DeviceIdType.MESH,
    )
    give.start()
    swaps[1].wait_recv()
    subtract(1, False)
    hand = pltpu.make_async_copy(left, left_out, store_sem.at[1])
    hand.start()
    give.wait_recv()
    w_out[...] = parts[...]
    received(2).wait_recv()
    received(NBLK).wait_recv()
    wh_out[...] = whole_half(NBLK - 1)
    for copy in copies + swaps + [give]:
        copy.wait_send()
    for k, sends in ((0, plane != PLANES - 1), (1, plane != 0)):
        @pl.when(sends)
        def _():
            for d in range(1, PLANES):
                slab_copy(k, plane, d).wait_send()

    for n in range(NBLK + 1):
        received(n).wait_send()
    keep.wait()
    hand.wait()


def exchange_call(order, bounds, phases, data, projections, targets):
    vmem = pl.BlockSpec(memory_space=pltpu.VMEM)
    smem = pl.BlockSpec(memory_space=pltpu.SMEM)
    hbm = pl.BlockSpec(memory_space=pl.ANY)
    rows, classes = targets.shape
    buffers = []
    for _, height, _ in CHUNKS:
        buffers += [
            pltpu.VMEM((height // 2, LANES), F32),
            pltpu.VMEM((height // 2, LANES), F32),
            pltpu.VMEM((2, 3, height // 16, LANES), F32),
            pltpu.VMEM((2, 3, height // 64, LANES), F32),
            pltpu.VMEM((height // 8, LANES), F32),
        ]
    dma = pltpu.SemaphoreType.DMA
    return pl.pallas_call(
        functools.partial(exchange_kernel, sine_coefficients(math.sqrt(2.0 / F))),
        in_specs=[smem, smem, vmem, hbm, hbm, hbm],
        out_specs=[vmem, vmem, hbm, hbm],
        out_shape=[
            pltpu.VMEM((2, NBLK, SLAB, LANES), F32),
            pltpu.VMEM((F, classes), BF),
            pltpu.VMEM((rows, F), BF),
            pltpu.VMEM((rows, classes), F32),
        ],
        scratch_shapes=[
            pltpu.VMEM(data.shape, BF),
            pltpu.VMEM(projections.shape, BF),
            pltpu.VMEM((data.shape[1], F), BF),
            pltpu.VMEM(targets.shape, BF),
            pltpu.VMEM((NBLK, rows, F), BF),
            pltpu.VMEM((rows, classes), F32),
            pltpu.VMEM((HEIGHT, LANES), F32),
            pltpu.VMEM((HEIGHT, LANES), F32),
            pltpu.VMEM((F, F), F32),
            pltpu.VMEM((PLANES, 2, CHIP_SLAB, F), F32),
            pltpu.VMEM((NBLK, 2, F, LANES), BF),
            pltpu.VMEM((2, NBLK, SLAB, LANES), F32),
            pltpu.VMEM((NBLK, SLAB, LANES), F32),
            *buffers,
            dma((len(CHUNKS), COPIES)),
            dma((len(CHUNKS), COPIES)),
            dma((2, PLANES)),
            dma((2, PLANES)),
            dma((NBLK + 1,)),
            dma((NBLK + 1,)),
            dma((NBLK,)),
            dma((NBLK,)),
            dma((2 + TILES,)),
            dma((2,)),
        ],
        compiler_params=pltpu.CompilerParams(collective_id=0, has_side_effects=True, vmem_limit_bytes=58500 << 10),
        name="exchange",
    )(order, bounds.T, phases, data, projections, targets)


def residual_kernel(order, w, feats, half, left, weights, residual, result, store_sem):
    for turn in range(NBLK):
        weights[order[turn]] = jnp.concatenate([w[0, turn], w[1, turn]], axis=1)
    stores = []
    for t in range(left.shape[0] // RESIDUAL_TILE):
        rows = pl.ds(t * RESIDUAL_TILE, RESIDUAL_TILE)
        product = jnp.dot(feats[rows, :], half[...], preferred_element_type=F32)
        result[rows, :] = left[rows, :] - product
        copy = pltpu.make_async_copy(result.at[rows], residual.at[rows], store_sem.at[t])
        copy.start()
        stores.append(copy)
    for copy in stores:
        copy.wait()


def residual_call(order, feats, half, left, w):
    rows, classes = left.shape
    vmem = pl.BlockSpec(memory_space=pltpu.VMEM)
    return pl.pallas_call(
        residual_kernel,
        in_specs=[pl.BlockSpec(memory_space=pltpu.SMEM), vmem, vmem, vmem, vmem],
        out_specs=[vmem, pl.BlockSpec(memory_space=pl.ANY)],
        out_shape=[
            jax.ShapeDtypeStruct((NBLK, SLAB, classes), F32),
            jax.ShapeDtypeStruct((rows, classes), F32),
        ],
        scratch_shapes=[
            pltpu.VMEM((rows, classes), F32),
            pltpu.SemaphoreType.DMA((rows // RESIDUAL_TILE,)),
        ],
        compiler_params=pltpu.CompilerParams(vmem_limit_bytes=24 << 20),
        name="residual",
    )(order, w, feats, half, left)


def body(data, projections, phases, targets, bounds, order):
    w, half, feats, left = exchange_call(order, bounds, phases, data, projections, targets)
    weights, residual = residual_call(order, feats, half, left, w)
    return (weights, residual)


def solution(mesh):
    return jax.shard_map(
        body,
        mesh=mesh,
        in_specs=(P("rows", None), P(), P(), P("rows", "cls"), P(), P()),
        out_specs=(P(None, "rows", "cls"), P("rows", "cls")),
        check_vma=False,
    )
```

```python
import functools
import math

import jax
import jax.numpy as jnp
from jax import lax
from jax.experimental import pallas as pl
from jax.experimental.pallas import tpu as pltpu
from jax.sharding import PartitionSpec as P

F = 512
NBLK = 3
TILE = 512
RESIDUAL_TILE = 1024
TILES = 4
SLAB = 16
BF = jnp.bfloat16
F32 = jnp.float32
LANES = 128
ROWS = 32
PLANES = 4
GRAM, CROSS, MOMENT, HEIGHT = 0, 3 * F, 7 * F, 13 * F
HALF = F // 2
TURN = 1.0 / (2.0 * math.pi)


def sine_coefficients(scale):
    import numpy as np

    nodes = np.cos((np.arange(64) + 0.5) * math.pi / 64)
    u = (nodes + 1) / 2 / 16
    a = np.sqrt(u)
    fit = np.polynomial.polynomial.polyfit(u, np.sin(2 * math.pi * a) / a, 3, w=a)
    return [float(c) * scale for c in fit]


def scaled_cosine(turns, coefficients):
    a = 0.25 - jnp.abs(turns - jnp.round(turns))
    u = a * a
    value = coefficients[-1]
    for c in coefficients[-2::-1]:
        value = value * u + c
    return value * a


def split(x):
    high = x.astype(BF)
    return high, (x - high.astype(F32)).astype(BF)


def dot3(left, right, dims=(((1,), (0,)), ((), ()))):
    lh, ll = left
    rh, rl = right
    dot = functools.partial(lax.dot_general, dimension_numbers=dims, preferred_element_type=F32)
    return dot(lh, rh) + (dot(lh, rl) + dot(ll, rh))


def mod4(v):
    return lax.rem(v + 8, 4)


class Place:
    def __init__(self):
        self.row = lax.axis_index("rows")
        self.plane = lax.axis_index("cls")
        self.core = lax.rem(self.row, 2)
        self.x = lax.rem(lax.div(self.row, 2), 4)
        self.y = lax.div(self.row, 8)
        self.partner = {"rows": self.row + 1 - 2 * self.core}

    def at(self, axis):
        return self.x if axis == "x" else self.y

    def near(self, axis, step):
        x = mod4(self.x + step) if axis == "x" else self.x
        y = mod4(self.y + step) if axis == "y" else self.y
        return {"rows": (y * 4 + x) * 2 + self.core}


def window(start, size):
    return pl.ds(pl.multiple_of(start, 8), size)


CHUNKS = (
    (GRAM, 3 * F, True),
    (CROSS, 4 * F, True),
    *((MOMENT + 2 * F * j, 2 * F, False) for j in range(NBLK)),
)
CHIP_SLAB = 2 * SLAB
CHIPS = ROWS // 2
COPIES = 27


def reduce_chunk(place, q, v, out, r0, acc, ring1, ring2, part1, send_sem, recv_sem, copies):
    base, height, join = CHUNKS[q]
    half = height // 2
    hops = [(part, d) for d in (2, 1, 3) for part in range(2)]

    def send(k, source, target, device):
        copy = pltpu.make_async_remote_copy(
            src_ref=source, dst_ref=target, send_sem=send_sem.at[q, k], recv_sem=recv_sem.at[q, k],
            device_id=device, device_id_type=pl.DeviceIdType.MESH,
        )
        copy.start()
        copies.append(copy)
        return copy

    first = send(0, v.at[window(base + (1 - place.core) * half, half)], r0, place.partner)
    yield
    first.wait_recv()
    acc[...] = v[window(base + place.core * half, half), :] + r0[...]

    def scatter(k, axes, source, origin, size, ring, store):
        flights = {}
        for part, d in hops:
            target = mod4(place.at(axes[part]) + d)
            piece = source.at[window(origin(part) + target * size, size)]
            flights[part, d] = send(k + part * 3 + d - 1, piece, ring.at[part, d - 1], place.near(axes[part], d))
        yield
        for part in range(2):
            total = source[window(origin(part) + place.at(axes[part]) * size, size), :]
            for d in range(1, 4):
                flights[part, d].wait_recv()
                total = total + ring[part, d - 1]
            store(part, total)

    def gather(k, axes, origin, size):
        flights = []
        for part, d in hops:
            mine = out.at[window(base + origin(part) + place.at(axes[part]) * size, size)]
            flights.append(send(k + part * 3 + d - 1, mine, mine, place.near(axes[part], d)))
        yield
        for copy in flights:
            copy.wait_recv()

    one, two = ("x", "y"), ("y", "x")
    quarter, sixteenth, last = height // 4, height // 16, height // 64

    def store1(part, value):
        part1[part * sixteenth:(part + 1) * sixteenth, :] = value

    yield from scatter(1, one, acc, lambda part: part * quarter, sixteenth, ring1, store1)

    def own(part):
        return place.core * half + part * quarter + place.at(one[part]) * sixteenth

    def store2(part, value):
        out[window(base + own(part) + place.at(two[part]) * last, last), :] = value

    yield from scatter(7, two, part1, lambda part: part * sixteenth, last, ring2, store2)
    yield from gather(13, two, own, last)
    yield from gather(19, one, lambda part: place.core * half + part * quarter, sixteenth)
    if not join:
        return
    finals = []
    for part in range(2):
        mine = out.at[window(base + place.core * half + part * quarter, quarter)]
        finals.append(send(25 + part, mine, mine, place.partner))
    yield
    for copy in finals:
        copy.wait_recv()


def exchange_kernel(
    coefficients, order, bounds, phases, data_in, proj_in, targets_in, w_out, wh_out, feats_out, left_out,
    data, proj, chosen, targets, feats, left, v, out, s1, slabs, wh, parts, other, *scratch
):
    place = Place()
    buffers = scratch[:5 * len(CHUNKS)]
    send_sem, recv_sem, plane_send, plane_recv, wide_send, wide_recv, pair_send, pair_recv, load_sem, store_sem = (
        scratch[5 * len(CHUNKS):]
    )
    me, plane = place.row, place.plane
    height = data.shape[0]
    loads = [pltpu.make_async_copy(proj_in, proj, load_sem.at[0])]
    for t in range(TILES):
        rows = pl.ds(t * TILE, TILE)
        loads.append(pltpu.make_async_copy(data_in.at[rows], data.at[rows], load_sem.at[1 + t]))
    loads.append(pltpu.make_async_copy(targets_in, targets, load_sem.at[1 + TILES]))
    for copy in loads[:3]:
        copy.start()

    barrier = pltpu.get_barrier_semaphore()

    greeted = [place.partner]
    greeted += [place.near(axis, d) for axis in ("x", "y") for d in range(1, 4)]
    greeted += [{"cls": lax.rem(plane + d, PLANES)} for d in range(1, PLANES)]
    for device in greeted:
        pl.semaphore_signal(barrier, inc=1, device_id=device, device_id_type=pl.DeviceIdType.MESH)

    copies = []
    runs = [
        reduce_chunk(place, q, v, out, *buffers[5 * q:5 * q + 5], send_sem, recv_sem, copies)
        for q in range(len(CHUNKS))
    ]
    done = [False] * len(runs)

    def advance(*which):
        for q in which:
            if not done[q]:
                try:
                    next(runs[q])
                except StopIteration:
                    done[q] = True

    turn_a = jnp.minimum(plane, 2)
    turn_b = jnp.where(plane == 0, 1, 0)
    turn_c = 3 - turn_a - turn_b
    turn_x = jnp.where(plane == 3, 1, 0)
    contract = (((0,), (0,)), ((), ()))

    def pick(turn, values):
        block = order[turn]
        return jnp.where(block == 0, values[0], jnp.where(block == 1, values[1], values[2]))

    def columns(ref):
        return [ref[:, j * F:(j + 1) * F] for j in range(NBLK)]

    def choose(turn):
        chosen[...] = pick(turn, columns(proj))

    def features(turn, tiles):
        shift = pick(turn, [phases[j * F:(j + 1) * F] for j in range(NBLK)])[None, :] * TURN
        for t in tiles:
            rows = pl.ds(t * TILE, TILE)
            angle = jnp.dot(data[rows, :], chosen[...], preferred_element_type=F32)
            feats[turn, rows, :] = scaled_cosine(angle * TURN + shift, coefficients).astype(BF)

    def put(base, value):
        tall, width = value.shape
        for k in range(width // LANES):
            v[window(base + k * tall, tall), :] = value[:, k * LANES:(k + 1) * LANES]

    def moments(turn):
        put(MOMENT + 2 * F * turn, lax.dot_general(feats[turn], targets[...], contract, preferred_element_type=F32))

    def gram():
        for n in range(2):
            lhs = feats[turn_a, :, n * HALF:(n + 1) * HALF]
            rhs = feats[turn_a, :, n * HALF:]
            put(GRAM + n * 2 * F, lax.dot_general(lhs, rhs, contract, preferred_element_type=F32))

    G, C, M0, M1, M2 = range(5)
    loads[0].wait()
    for copy in loads[3:]:
        copy.start()
    choose(turn_a)
    for t in range(TILES):
        loads[1 + t].wait()
        features(turn_a, [t])
    gram()
    pl.semaphore_wait(barrier, len(greeted))
    choose(turn_b)
    features(turn_b, [0])
    advance(G)
    features(turn_b, [1])
    features(turn_b, [2])
    features(turn_b, [3])
    advance(G)
    loads[1 + TILES].wait()
    moments(0)
    choose(turn_c)
    features(turn_c, [0])
    advance(M0)
    features(turn_c, [1])
    features(turn_c, [2])
    features(turn_c, [3])
    put(CROSS, lax.dot_general(feats[turn_a], feats[turn_x], contract, preferred_element_type=F32))
    advance(C, M0)
    moments(1)
    advance(M1, G, C, M0, G, M1, C, M0, G)
    moments(2)
    keep = pltpu.make_async_copy(feats.at[NBLK - 1], feats_out, store_sem.at[0])
    keep.start()
    advance(M2, M1, C, M2, M0, G, M1, C, G)

    def wide(base, width, tall=F):
        return jnp.concatenate([out[window(base + k * tall, tall), :] for k in range(width // LANES)], axis=1)

    lower = jnp.full((1, F), pick(turn_a, [bounds[0, j] for j in range(NBLK)]), F32)
    upper = jnp.full((1, F), pick(turn_a, [bounds[1, j] for j in range(NBLK)]), F32)
    center = 0.5 * (upper + lower)
    u = 0.5 * (upper - lower) / center
    k1 = 2.0 / (2.0 - u * u)
    u = u * u / (2.0 - u * u)
    k2 = 2.0 / (2.0 - u * u)
    u = u * u / (2.0 - u * u)
    k4 = 2.0 / (2.0 - u * u)
    u = u * u / (2.0 - u * u)
    k8 = 2.0 / (2.0 - u * u)
    scale = 1.0 / (center * (height * ROWS))

    eye = (
        lax.broadcasted_iota(jnp.int32, (F, F), 0) == lax.broadcasted_iota(jnp.int32, (F, F), 1)
    ).astype(F32)
    top = wide(GRAM, F, HALF)
    corner = wide(GRAM + 2 * F, HALF, HALF)
    whole = jnp.concatenate([top, jnp.concatenate([top[:, HALF:].T, corner], axis=1)], axis=0)
    first = whole * scale + eye * (lower / center)
    s1[...] = first
    chip = lax.div(me, 2)
    row = lax.broadcasted_iota(jnp.int32, (CHIP_SLAB, F), 0) + chip * CHIP_SLAB
    column = lax.broadcasted_iota(jnp.int32, (CHIP_SLAB, F), 1)
    unit = (row == column).astype(F32)
    value = k1 * (2.0 * unit - s1[window(chip * CHIP_SLAB, CHIP_SLAB), :])
    part1 = split(first)
    second = k1 * (2.0 * first - dot3(part1, part1))
    part2 = split(second)
    value = k2 * (2.0 * value - dot3(split(value), part2))
    fourth = k2 * (2.0 * second - dot3(part2, part2))
    part4 = split(fourth)
    value = k4 * (2.0 * value - dot3(split(value), part4))
    once = dot3(split(value), part4)
    value = k8 * (2.0 * value - k4 * (2.0 * once - dot3(split(once), part4)))
    value = value * scale

    inner = jnp.logical_and(plane != 0, plane != PLANES - 1)
    edge = plane == 0

    def slab_copy(k, source, d):
        return pltpu.make_async_remote_copy(
            src_ref=slabs.at[source, k], dst_ref=slabs.at[source, k],
            send_sem=plane_send.at[k, d], recv_sem=plane_recv.at[k, source],
            device_id={"cls": lax.rem(plane + d, PLANES)}, device_id_type=pl.DeviceIdType.MESH,
        )

    def cross_planes(k, sends):
        @pl.when(sends)
        def _():
            for d in (2, 1, 3):
                slab_copy(k, plane, d).start()

    def arrived(k, source):
        @pl.when(plane != source)
        def _():
            slab_copy(k, source, 1).wait_recv()

    slabs[plane, 0] = value
    cross_planes(0, edge)
    advance(M2, M0, M1, C, M2, C)
    slabs[plane, 1] = dot3(split(value), split(wide(CROSS, F)))
    cross_planes(1, plane != 0)
    cross_planes(0, inner)

    def moment(j):
        return split(out[window(MOMENT + 2 * F * j + place.core * F, F), :])

    def product(z, k, right):
        return dot3(split(slabs[z, k]), right)

    def product2(z, k, right):
        high, low = split(slabs[z, k])
        return jnp.dot(high, right, preferred_element_type=F32) + jnp.dot(low, right, preferred_element_type=F32)

    def half(j):
        return wh[j, place.core]

    def pair_copy(n, ref):
        return pltpu.make_async_remote_copy(
            src_ref=ref, dst_ref=ref, send_sem=pair_send.at[n], recv_sem=pair_recv.at[n],
            device_id=place.partner, device_id_type=pl.DeviceIdType.MESH,
        )

    far_first = sorted(
        ((dx, dy) for dx in range(4) for dy in range(4)),
        key=lambda hop: -(min(hop[0], 4 - hop[0]) + min(hop[1], 4 - hop[1])),
    )

    def broadcast(j, w):
        parts[place.core, j] = w[:SLAB]
        other[j] = w[SLAB:]

        @pl.when(place.core == 1)
        def _():
            parts[place.core, j] = w[SLAB:]
            other[j] = w[:SLAB]

        mine = wh.at[j, place.core, pl.ds(pl.multiple_of(chip * CHIP_SLAB, CHIP_SLAB), CHIP_SLAB)]
        wh[j, place.core, pl.ds(pl.multiple_of(chip * CHIP_SLAB, CHIP_SLAB), CHIP_SLAB), :] = w.astype(BF)
        for dx, dy in far_first:
            there = (mod4(place.y + dy) * 4 + mod4(place.x + dx)) * 2
            for swap in range(2 if j == NBLK - 1 else 1):
                if dx == 0 and dy == 0 and swap == 0:
                    continue
                core = 1 - place.core if swap else place.core
                pltpu.make_async_remote_copy(
                    src_ref=mine, dst_ref=mine, send_sem=wide_send.at[j + swap], recv_sem=wide_recv.at[j + swap],
                    device_id={"rows": there + core}, device_id_type=pl.DeviceIdType.MESH,
                ).start()

    def received(n):
        j = min(n, NBLK - 1)
        part = wh.at[j, 0, pl.ds(0, F if n == NBLK else F - CHIP_SLAB)]
        return pltpu.make_async_remote_copy(
            src_ref=part, dst_ref=part, send_sem=wide_send.at[n], recv_sem=wide_recv.at[n],
            device_id=place.partner, device_id_type=pl.DeviceIdType.MESH,
        )

    def whole_half(j):
        return jnp.concatenate([wh[j, 0], wh[j, 1]], axis=1)

    def subtract(turn, start):
        both = whole_half(turn)
        for t in range(TILES):
            rows = pl.ds(t * TILE, TILE)
            before = targets[rows, :].astype(F32) if start else left[rows, :]
            left[rows, :] = before - jnp.dot(feats[turn, rows, :], both, preferred_element_type=F32)

    arrived(0, 0)
    broadcast(0, product(0, 0, moment(0)))
    advance(M1, M2)
    arrived(0, 1)
    w1 = product(1, 0, moment(1))
    for source in range(1, PLANES):
        arrived(1, source)
    received(0).wait_recv()
    w1 = w1 - product2(1, 1, half(0))
    broadcast(1, w1)
    advance(M2)
    assert all(done)
    swaps = [pair_copy(0, wh.at[0, place.core])]
    swaps[0].start()
    arrived(0, 2)
    w2 = product(2, 0, moment(2)) - product2(2, 1, half(0))
    swaps[0].wait_recv()
    subtract(0, True)
    received(1).wait_recv()
    broadcast(2, w2 - product2(3, 1, half(1)))
    swaps.append(pair_copy(1, wh.at[1, place.core]))
    swaps[1].start()
    give = pltpu.make_async_remote_copy(
        src_ref=other, dst_ref=parts.at[place.core], send_sem=pair_send.at[2], recv_sem=pair_recv.at[2],
        device_id=place.partner, device_id_type=pl.DeviceIdType.MESH,
    )
    give.start()
    swaps[1].wait_recv()
    subtract(1, False)
    hand = pltpu.make_async_copy(left, left_out, store_sem.at[1])
    hand.start()
    give.wait_recv()
    w_out[...] = parts[...]
    received(2).wait_recv()
    received(NBLK).wait_recv()
    wh_out[...] = whole_half(NBLK - 1)
    for copy in copies + swaps + [give]:
        copy.wait_send()
    for k, sends in ((0, plane != PLANES - 1), (1, plane != 0)):
        @pl.when(sends)
        def _():
            for d in range(1, PLANES):
                slab_copy(k, plane, d).wait_send()

    for n in range(NBLK + 1):
        received(n).wait_send()
    keep.wait()
    hand.wait()


def exchange_call(order, bounds, phases, data, projections, targets):
    vmem = pl.BlockSpec(memory_space=pltpu.VMEM)
    smem = pl.BlockSpec(memory_space=pltpu.SMEM)
    hbm = pl.BlockSpec(memory_space=pl.ANY)
    rows, classes = targets.shape
    buffers = []
    for _, height, _ in CHUNKS:
        buffers += [
            pltpu.VMEM((height // 2, LANES), F32),
            pltpu.VMEM((height // 2, LANES), F32),
            pltpu.VMEM((2, 3, height // 16, LANES), F32),
            pltpu.VMEM((2, 3, height // 64, LANES), F32),
            pltpu.VMEM((height // 8, LANES), F32),
        ]
    dma = pltpu.SemaphoreType.DMA
    return pl.pallas_call(
        functools.partial(exchange_kernel, sine_coefficients(math.sqrt(2.0 / F))),
        in_specs=[smem, smem, vmem, hbm, hbm, hbm],
        out_specs=[vmem, vmem, hbm, hbm],
        out_shape=[
            pltpu.VMEM((2, NBLK, SLAB, LANES), F32),
            pltpu.VMEM((F, classes), BF),
            pltpu.VMEM((rows, F), BF),
            pltpu.VMEM((rows, classes), F32),
        ],
        scratch_shapes=[
            pltpu.VMEM(data.shape, BF),
            pltpu.VMEM(projections.shape, BF),
            pltpu.VMEM((data.shape[1], F), BF),
            pltpu.VMEM(targets.shape, BF),
            pltpu.VMEM((NBLK, rows, F), BF),
            pltpu.VMEM((rows, classes), F32),
            pltpu.VMEM((HEIGHT, LANES), F32),
            pltpu.VMEM((HEIGHT, LANES), F32),
            pltpu.VMEM((F, F), F32),
            pltpu.VMEM((PLANES, 2, CHIP_SLAB, F), F32),
            pltpu.VMEM((NBLK, 2, F, LANES), BF),
            pltpu.VMEM((2, NBLK, SLAB, LANES), F32),
            pltpu.VMEM((NBLK, SLAB, LANES), F32),
            *buffers,
            dma((len(CHUNKS), COPIES)),
            dma((len(CHUNKS), COPIES)),
            dma((2, PLANES)),
            dma((2, PLANES)),
            dma((NBLK + 1,)),
            dma((NBLK + 1,)),
            dma((NBLK,)),
            dma((NBLK,)),
            dma((2 + TILES,)),
            dma((2,)),
        ],
        compiler_params=pltpu.CompilerParams(collective_id=0, has_side_effects=True, vmem_limit_bytes=58500 << 10),
        name="exchange",
    )(order, bounds.T, phases, data, projections, targets)


def residual_kernel(order, w, feats, half, left, weights, residual, result, store_sem):
    for turn in range(NBLK):
        weights[order[turn]] = jnp.concatenate([w[0, turn], w[1, turn]], axis=1)
    stores = []
    for t in range(left.shape[0] // RESIDUAL_TILE):
        rows = pl.ds(t * RESIDUAL_TILE, RESIDUAL_TILE)
        product = jnp.dot(feats[rows, :], half[...], preferred_element_type=F32)
        result[rows, :] = left[rows, :] - product
        copy = pltpu.make_async_copy(result.at[rows], residual.at[rows], store_sem.at[t])
        copy.start()
        stores.append(copy)
    for copy in stores:
        copy.wait()


def residual_call(order, feats, half, left, w):
    rows, classes = left.shape
    vmem = pl.BlockSpec(memory_space=pltpu.VMEM)
    return pl.pallas_call(
        residual_kernel,
        in_specs=[pl.BlockSpec(memory_space=pltpu.SMEM), vmem, vmem, vmem, vmem],
        out_specs=[vmem, pl.BlockSpec(memory_space=pl.ANY)],
        out_shape=[
            jax.ShapeDtypeStruct((NBLK, SLAB, classes), F32),
            jax.ShapeDtypeStruct((rows, classes), F32),
        ],
        scratch_shapes=[
            pltpu.VMEM((rows, classes), F32),
            pltpu.SemaphoreType.DMA((rows // RESIDUAL_TILE,)),
        ],
        compiler_params=pltpu.CompilerParams(vmem_limit_bytes=24 << 20),
        name="residual",
    )(order, w, feats, half, left)


def body(data, projections, phases, targets, bounds, order):
    w, half, feats, left = exchange_call(order, bounds, phases, data, projections, targets)
    weights, residual = residual_call(order, feats, half, left, w)
    return (weights, residual)


def solution(mesh):
    return jax.shard_map(
        body,
        mesh=mesh,
        in_specs=(P("rows", None), P(), P(), P("rows", "cls"), P(), P()),
        out_specs=(P(None, "rows", "cls"), P("rows", "cls")),
        check_vma=False,
    )
```
